128 devices in a mesh: grp: 4 (over y), blk: 8 (over z, x_lo), ch: 4 (over x_hi, core).
Axes of the slice: x: 4 (x_hi: 2, x_lo: 2; x = x_hi * 2 + x_lo), y: 4, z: 4, core: 2. Of those that a mesh axis runs over, the one named last changes fastest.
Arguments:
- gate_in: bfloat16 [12288, 1024], P(('grp', 'blk'), 'ch'), parts along dimension 1, may hold values from -6 to 6
- value_in: bfloat16 [12288, 1024], P(('grp', 'blk'), 'ch'), parts along dimension 1, may hold values from -6 to 6
- gate_out: bfloat16 [12288, 1024], P(('grp', 'blk'), 'ch'), parts along dimension 1, may hold values from -6 to 6
- filter_taps: float32 [12288, 1024], P(('grp', 'blk'), 'ch'), parts along dimension 1, may hold values from -6 to 6
- skip_gain: float32 [1024], P('ch'), parts along dimension 0, may hold values from -4 to 4
- cotangent: bfloat16 [12288, 1024], P(('grp', 'blk'), 'ch'), parts along dimension 1, may hold values from -10 to 10
Outputs:
- grad_gate_in: bfloat16 [12288, 1024], P(('grp', 'blk'), 'ch'), parts along dimension 1
- grad_value_in: bfloat16 [12288, 1024], P(('grp', 'blk'), 'ch'), parts along dimension 1
- grad_gate_out: bfloat16 [12288, 1024], P(('grp', 'blk'), 'ch'), parts along dimension 1
- grad_filter: float32 [12288, 1024], P(('grp', 'blk'), 'ch'), parts along dimension 1
- grad_skip: float32 [1024], P('ch'), parts along dimension 0
The draws below stay inside these ranges and needn't reach their ends.
There are 4 independent parts, one for each index of `ch`. The reference program is written for one: setup_inputs(seed, part) draws one part's arguments, and reference() takes and returns one part's arrays. A program takes and returns all parts, laid end to end along the dimension named above; each array names one. Nothing has to cross between parts.
All inputs are finite; a program needn't handle non-finite values.
Results may differ from the reference program's by a relative error of at most 0.001.
Values sent between devices are 32-bit elements; how exact they have to be, the bound alone decides.
No kernel may reach another device: no remote copies, remote signals or barrier semaphores. Data moves between devices by JAX's collectives and lax.ppermute only.
A program may use at most 128 MiB of HBM per device.

```python
import math
import jax
import jax.numpy as jnp
from jax import lax

C = 256
SEQUENCE_TOKENS = 12288


def draw_filter_taps(key, part):
    random_keys = jax.random.split(key, 6)
    step_offsets = jnp.arange(SEQUENCE_TOKENS, dtype=jnp.float32)[:, None]
    noise = jax.random.truncated_normal(random_keys[1], -5.0, 5.0, (SEQUENCE_TOKENS, C), jnp.float32)
    slow_share = 5
    slow = jax.random.randint(random_keys[0], (C,), 0, 10) < slow_share
    fast_rate = 1.0 / (30.0 + 20.0 * jax.random.uniform(random_keys[2], (C,), jnp.float32))
    slow_rate = jnp.exp(jax.random.uniform(random_keys[3], (C,), jnp.float32, math.log(0.1), math.log(0.5))) / SEQUENCE_TOKENS
    decay_speed = jnp.where(slow, slow_rate, fast_rate)
    decay_pulses = jax.random.randint(random_keys[4], (2,), 1, SEQUENCE_TOKENS)
    decay_falloffs = jax.random.uniform(random_keys[5], (2,), jnp.float32, 0.6, 0.8)
    token_position = jnp.arange(SEQUENCE_TOKENS, dtype=jnp.int32)[:, None]
    decay_pulse = jnp.prod(jnp.where(token_position >= decay_pulses[None, :], decay_falloffs[None, :], 1.0), axis=1)
    decay_window = jnp.exp(-decay_speed[None, :] * step_offsets) * decay_pulse[:, None]
    norm = jnp.sqrt((1.0 - jnp.exp(-2.0 * decay_speed * SEQUENCE_TOKENS)) / (1.0 - jnp.exp(-2.0 * decay_speed)))
    taps = noise * decay_window / norm[None, :]
    return taps.astype(jnp.float32)


def draw_cotangent(key, part):
    ramp = jnp.arange(SEQUENCE_TOKENS, dtype=jnp.float32)[:, None] / (SEQUENCE_TOKENS - 1)
    base = jax.random.truncated_normal(key, -5.0, 5.0, (SEQUENCE_TOKENS, C), jnp.float32)
    decay_window = 0.5 + 1.5 * ramp
    return (base * decay_window).astype(jnp.bfloat16)


def block_levels(stream_key, shape, pieces, smallest, high):
    level = 1.0
    for axis_at, blocks in pieces:
        heights = jax.random.uniform(jax.random.fold_in(jax.random.fold_in(stream_key, 6), axis_at), (blocks,), jnp.float32, smallest / len(pieces), high / len(pieces))
        level = level * jnp.repeat(jnp.exp(heights), shape[axis_at] // blocks).reshape((-1,) + (1,) * (len(shape) - 1 - axis_at))
    return level


def centred(key, shape, width, most, pieces=(), kind=jnp.bfloat16):
    gain = block_levels(key, shape, pieces, -0.22, 0.18) if pieces else 1.0
    values = jax.random.normal(key, shape, jnp.float32) * width * gain
    return jnp.minimum(jnp.maximum(values, -most), most).astype(kind)


def setup_inputs(seed: int = 0, part: int = 0) -> dict:
    splits = jax.random.split(jax.random.key(seed), 7)
    part_keys = jax.random.split(jax.random.fold_in(splits[6], part), 7)
    gate_in = centred(part_keys[0], (SEQUENCE_TOKENS, C), 1.0, 6.0, ((0, 32),))
    value_in = centred(part_keys[1], (SEQUENCE_TOKENS, C), 1.0, 6.0, ((0, 32),))
    gate_out = centred(part_keys[2], (SEQUENCE_TOKENS, C), 1.0, 6.0, ((0, 32),))
    filter_taps = draw_filter_taps(jax.random.fold_in(jax.random.fold_in(splits[6], part), 71), part)
    skip_gain = centred(part_keys[4], (C,), 1.0, 4.0, (), jnp.float32)
    cotangent = draw_cotangent(jax.random.fold_in(jax.random.fold_in(splits[6], part), 71), part)
    return {"gate_in": gate_in, "value_in": value_in, "gate_out": gate_out, "filter_taps": filter_taps, "skip_gain": skip_gain, "cotangent": cotangent}


def reference(gate_in, value_in, gate_out, filter_taps, skip_gain, cotangent):
    first = gate_in.astype(jnp.float32)
    value = value_in.astype(jnp.float32)
    second = gate_out.astype(jnp.float32)
    grad = cotangent.astype(jnp.float32)
    mixed = first * value
    upstream = grad * second
    total = 2 * SEQUENCE_TOKENS
    spec_mixed = jnp.fft.rfft(mixed, n=total, axis=0)
    spec_filter = jnp.fft.rfft(filter_taps, n=total, axis=0)
    spec_up = jnp.fft.rfft(upstream, n=total, axis=0)
    conv = jnp.fft.irfft(spec_filter * spec_mixed, n=total, axis=0)[:SEQUENCE_TOKENS]
    back = jnp.fft.irfft(jnp.conj(spec_filter) * spec_up, n=total, axis=0)[:SEQUENCE_TOKENS]
    lagged = jnp.fft.irfft(jnp.conj(spec_mixed) * spec_up, n=total, axis=0)[:SEQUENCE_TOKENS]
    scale = 1.0 / math.sqrt(SEQUENCE_TOKENS)
    grad_gate_out = (grad * (conv + skip_gain[None, :] * mixed)).astype(jnp.bfloat16)
    grad_mixed = back + skip_gain[None, :] * upstream
    grad_gate_in = (grad_mixed * value).astype(jnp.bfloat16)
    grad_value_in = (grad_mixed * first).astype(jnp.bfloat16)
    grad_filter = (lagged * scale).astype(jnp.float32)
    grad_skip = (lax.optimization_barrier(jnp.sum(upstream * mixed, axis=0)) * scale).astype(jnp.float32)
    return (grad_gate_in, grad_value_in, grad_gate_out, grad_filter, grad_skip)
```

```python
import math

import jax
import jax.numpy as jnp
import numpy as np
from jax import lax
from jax.experimental import pallas as pl
from jax.experimental.pallas import tpu as pltpu
from jax.sharding import PartitionSpec as P

AXES = ("grp", "blk")
LANES = 128
SUB = 8
INTERPRET = False


def split_table(table):
    high = table.astype(jnp.bfloat16)
    low = (table - high.astype(np.float64)).astype(jnp.bfloat16)
    return np.stack([high, low])


def tables(blocks, radix):
    total = blocks * radix * LANES
    eye = np.eye(SUB)
    near = np.arange(blocks)
    outer = 2.0 * np.pi * np.outer(near + 0.25, near) / blocks
    parts = np.stack([np.cos(outer), -np.sin(outer)])
    ahead = np.einsum("pkd,ce->pckde", parts, eye).reshape(2 * SUB * blocks, blocks * SUB)
    behind = ahead.T / total
    lane = np.arange(LANES)
    inner = 2.0 * np.pi * np.outer(lane, lane) / LANES
    cosine, sine = np.cos(inner), np.sin(inner)
    lane_ahead = np.block([[cosine, -sine], [sine, cosine]])
    lane_behind = np.block([[cosine, sine], [-sine, cosine]])
    piece = np.arange(radix)
    turn = 2.0 * np.pi * piece[:, None] * (near[None, :] + 0.25) / (blocks * radix)
    turn = np.broadcast_to(turn[:, :, None], (radix, blocks, LANES))
    key = near[None, :] + blocks * piece[:, None] + 0.25
    fine = 2.0 * np.pi * key[:, :, None] * lane[None, None, :] / total
    angles = np.stack([turn, fine])
    twist = np.stack([np.cos(angles), np.sin(angles)], axis=1).astype(np.float32)
    return (
        split_table(ahead),
        split_table(lane_ahead),
        split_table(lane_behind),
        split_table(behind),
        twist,
    )


def halves(values):
    high = values.astype(jnp.bfloat16)
    low = (values - high.astype(jnp.float32)).astype(jnp.bfloat16)
    return high, low


def dot(a, b):
    return jnp.dot(a, b, preferred_element_type=jnp.float32)


def pack_kernel(gate_in, value_in, gate_out, cotangent, taps, out):
    signals = (
        gate_in[...].astype(jnp.float32) * value_in[...].astype(jnp.float32),
        taps[...],
        cotangent[...].astype(jnp.float32) * gate_out[...].astype(jnp.float32),
    )
    radix = signals[0].shape[0] // LANES
    for s, signal in enumerate(signals):
        for a in range(radix):
            turned = signal[a * LANES : (a + 1) * LANES].T
            at = (a * 3 + s) * SUB
            out[:, at : at + SUB, :] = turned.reshape(-1, SUB, LANES)


def spectral_kernel(
    data, ahead, lane_ahead, lane_behind, behind, twist, out, xs, fs, gs, spec, gain
):
    blocks = data.shape[0]
    radix = twist.shape[2]
    half_root = math.sqrt(0.75)
    width = radix * LANES
    total = jnp.zeros((SUB, LANES), jnp.float32)
    for s in range(3):
        for a in range(radix):
            at = (a * 3 + s) * SUB
            high, low = halves(data[:, at : at + SUB, :].reshape(blocks * SUB, LANES))
            to = s * width + a * LANES
            xs[0, :, to : to + LANES] = high
            xs[1, :, to : to + LANES] = low
    for a in range(radix):
        mixed = data[:, a * 3 * SUB : a * 3 * SUB + SUB, :]
        up = data[:, (a * 3 + 2) * SUB : (a * 3 + 3) * SUB, :]
        total = total + jnp.sum(mixed * up, axis=0)
    skip_at = 3 * radix * SUB
    out[:, skip_at : skip_at + SUB, :] = jnp.broadcast_to(total[None], (blocks, SUB, LANES))

    first = dot(ahead[0], xs[0]) + dot(ahead[0], xs[1]) + dot(ahead[1], xs[0])
    fs[...] = first.reshape(2, SUB, blocks, 3 * width)

    for s in range(3):

        def forward(c, _, s=s):
            real, imag = [], []
            for a in range(radix):
                at = s * width + a * LANES
                re = fs[0, c, :, at : at + LANES]
                im = fs[1, c, :, at : at + LANES]
                if a:
                    co = twist[0, 0, a]
                    si = twist[0, 1, a]
                    re, im = re * co + im * si, im * co - re * si
                real.append(re)
                imag.append(im)
            sum_re, sum_im = real[1] + real[2], imag[1] + imag[2]
            mid_re, mid_im = real[0] - 0.5 * sum_re, imag[0] - 0.5 * sum_im
            dif_re = half_root * (real[1] - real[2])
            dif_im = half_root * (imag[1] - imag[2])
            outs = (
                (real[0] + sum_re, imag[0] + sum_im),
                (mid_re + dif_im, mid_im - dif_re),
                (mid_re - dif_im, mid_im + dif_re),
            )
            for e, (re, im) in enumerate(outs):
                co = twist[1, 0, e]
                si = twist[1, 1, e]
                for p, v in enumerate((re * co + im * si, im * co - re * si)):
                    high, low = halves(v)
                    gs[0, s, e, c, :, p * LANES : (p + 1) * LANES] = high
                    gs[1, s, e, c, :, p * LANES : (p + 1) * LANES] = low
            return 0

        lax.fori_loop(0, SUB, forward, 0)
        rows = radix * SUB * blocks
        high = gs[0, s].reshape(rows, 2 * LANES)
        low = gs[1, s].reshape(rows, 2 * LANES)
        result = dot(high, lane_ahead[0]) + dot(low, lane_ahead[0]) + dot(high, lane_ahead[1])
        spec[s] = result.reshape(radix, SUB, blocks, 2 * LANES)

    def product(c, _):
        for e in range(radix):
            mr, mi = spec[0, e, c, :, :LANES], spec[0, e, c, :, LANES:]
            hr, hi = spec[1, e, c, :, :LANES], spec[1, e, c, :, LANES:]
            ur, ui = spec[2, e, c, :, :LANES], spec[2, e, c, :, LANES:]
            outs = (
                (hr * mr - hi * mi, hr * mi + hi * mr),
                (hr * ur + hi * ui, hr * ui - hi * ur),
                (mr * ur + mi * ui, mr * ui - mi * ur),
            )
            for s, pair in enumerate(outs):
                for p, v in enumerate(pair):
                    high, low = halves(v)
                    gs[0, s, e, c, :, p * LANES : (p + 1) * LANES] = high
                    gs[1, s, e, c, :, p * LANES : (p + 1) * LANES] = low
        return 0

    lax.fori_loop(0, SUB, product, 0)

    for s in range(3):
        rows = radix * SUB * blocks
        high = gs[0, s].reshape(rows, 2 * LANES)
        low = gs[1, s].reshape(rows, 2 * LANES)
        result = dot(high, lane_behind[0]) + dot(low, lane_behind[0]) + dot(high, lane_behind[1])
        spec[s] = result.reshape(radix, SUB, blocks, 2 * LANES)

        def backward(c, _, s=s):
            real, imag = [], []
            for e in range(radix):
                re, im = spec[s, e, c, :, :LANES], spec[s, e, c, :, LANES:]
                co = twist[1, 0, e]
                si = twist[1, 1, e]
                real.append(re * co - im * si)
                imag.append(im * co + re * si)
            sum_re, sum_im = real[1] + real[2], imag[1] + imag[2]
            mid_re, mid_im = real[0] - 0.5 * sum_re, imag[0] - 0.5 * sum_im
            dif_re = half_root * (real[1] - real[2])
            dif_im = half_root * (imag[1] - imag[2])
            outs = (
                (real[0] + sum_re, imag[0] + sum_im),
                (mid_re - dif_im, mid_im + dif_re),
                (mid_re + dif_im, mid_im - dif_re),
            )
            for a, (re, im) in enumerate(outs):
                if a:
                    co = twist[0, 0, a]
                    si = twist[0, 1, a]
                    re, im = re * co - im * si, im * co + re * si
                at = s * width + a * LANES
                for p, v in enumerate((re, im)):
                    high, low = halves(v)
                    gain[0, p, c, :, at : at + LANES] = high
                    gain[1, p, c, :, at : at + LANES] = low
            return 0

        lax.fori_loop(0, SUB, backward, 0)

    rows = 2 * SUB * blocks
    high = gain[0].reshape(rows, 3 * width)
    low = gain[1].reshape(rows, 3 * width)
    result = dot(behind[0], high) + dot(behind[0], low) + dot(behind[1], high)
    for s in range(3):
        for a in range(radix):
            at = (a * 3 + s) * SUB
            to = s * width + a * LANES
            out[:, at : at + SUB, :] = result[:, to : to + LANES].reshape(blocks, SUB, LANES)


def unpack_kernel(
    data, gate_in, value_in, gate_out, cotangent, skip_gain, g_in, g_value, g_out, g_taps, g_skip, *, scale
):
    channels = gate_in.shape[1]
    radix = gate_in.shape[0] // LANES
    gain = skip_gain[...]
    for a in range(radix):
        rows = slice(a * LANES, (a + 1) * LANES)
        conv, back, lagged = (
            data[:, (a * 3 + s) * SUB : (a * 3 + s + 1) * SUB, :].reshape(channels, LANES).T
            for s in range(3)
        )
        first = gate_in[rows, :].astype(jnp.float32)
        value = value_in[rows, :].astype(jnp.float32)
        second = gate_out[rows, :].astype(jnp.float32)
        grad = cotangent[rows, :].astype(jnp.float32)
        g_out[rows, :] = (grad * (conv + gain * (first * value))).astype(g_out.dtype)
        mid = back + gain * (grad * second)
        g_in[rows, :] = (mid * value).astype(g_in.dtype)
        g_value[rows, :] = (mid * first).astype(g_value.dtype)
        g_taps[rows, :] = lagged * scale
    at = 3 * radix * SUB
    share = data[:, at : at + SUB, :].reshape(channels, LANES).T
    g_skip[...] = jnp.sum(share, axis=0, keepdims=True) * scale


PARAMS = pltpu.CompilerParams(vmem_limit_bytes=56 * 1024 * 1024)


def call(kernel, out_shape, scratch=()):
    return pl.pallas_call(
        kernel, out_shape=out_shape, scratch_shapes=scratch, compiler_params=PARAMS, interpret=INTERPRET
    )


def pack(gate_in, value_in, gate_out, cotangent, taps):
    rows, channels = taps.shape
    height = 3 * rows // LANES * SUB
    shape = jax.ShapeDtypeStruct((channels // SUB, height, LANES), jnp.float32)
    return call(pack_kernel, shape)(gate_in, value_in, gate_out, cotangent, taps)


def spectral(data):
    blocks = data.shape[0]
    radix = data.shape[1] // (3 * SUB)
    width = radix * LANES
    consts = [jnp.asarray(t) for t in tables(blocks, radix)]
    shape = jax.ShapeDtypeStruct((blocks, (3 * radix + 1) * SUB, LANES), jnp.float32)
    scratch = [
        pltpu.VMEM((2, blocks * SUB, 3 * width), jnp.bfloat16),
        pltpu.VMEM((2, SUB, blocks, 3 * width), jnp.float32),
        pltpu.VMEM((2, 3, radix, SUB, blocks, 2 * LANES), jnp.bfloat16),
        pltpu.VMEM((3, radix, SUB, blocks, 2 * LANES), jnp.float32),
        pltpu.VMEM((2, 2, SUB, blocks, 3 * width), jnp.bfloat16),
    ]
    return call(spectral_kernel, shape, scratch)(data, *consts)


def unpack(data, gate_in, value_in, gate_out, cotangent, skip_gain, scale):
    rows, channels = gate_in.shape
    half = jax.ShapeDtypeStruct((rows, channels), jnp.bfloat16)
    shapes = (
        half,
        half,
        half,
        jax.ShapeDtypeStruct((rows, channels), jnp.float32),
        jax.ShapeDtypeStruct((1, channels), jnp.float32),
    )

    def kernel(*refs):
        unpack_kernel(*refs, scale=scale)

    outs = call(kernel, shapes)(data, gate_in, value_in, gate_out, cotangent, skip_gain[None])
    return (*outs[:4], outs[4][0])


def body(gate_in, value_in, gate_out, filter_taps, skip_gain, cotangent):
    scale = 1.0 / math.sqrt(lax.axis_size(AXES) * gate_in.shape[0])
    data = pack(gate_in, value_in, gate_out, cotangent, filter_taps)
    data = lax.all_to_all(data, AXES, split_axis=0, concat_axis=0, tiled=True)
    data = spectral(data)
    data = lax.all_to_all(data, AXES, split_axis=0, concat_axis=0, tiled=True)
    return unpack(data, gate_in, value_in, gate_out, cotangent, skip_gain, scale)


def solution(mesh):
    spread = P(AXES, "ch")
    return jax.shard_map(
        body,
        mesh=mesh,
        in_specs=(spread, spread, spread, spread, P("ch"), spread),
        out_specs=(spread, spread, spread, spread, P("ch")),
        check_vma=False,
    )
```

```python
import math

import jax
import jax.numpy as jnp
import numpy as np
from jax import lax
from jax.experimental import pallas as pl
from jax.experimental.pallas import tpu as pltpu
from jax.sharding import PartitionSpec as P

AXES = ("grp", "blk")
LANES = 128
SUB = 8
INTERPRET = False


def split_table(table, axis):
    high = table.astype(jnp.bfloat16)
    low = (table - high.astype(np.float64)).astype(jnp.bfloat16)
    return np.concatenate([high, high, low], axis=axis)


def tables(blocks, radix):
    total = blocks * radix * LANES
    eye = np.eye(SUB)
    near = np.arange(blocks)
    outer = 2.0 * np.pi * np.outer(near + 0.25, near) / blocks
    parts = np.stack([np.cos(outer), -np.sin(outer)])
    ahead = np.einsum("pkd,ce->pckde", parts, eye).reshape(2 * SUB * blocks, blocks * SUB)
    behind = ahead.T / total
    lane = np.arange(LANES)
    inner = 2.0 * np.pi * np.outer(lane, lane) / LANES
    cosine, sine = np.cos(inner), np.sin(inner)
    lane_ahead = np.block([[cosine, -sine], [sine, cosine]])
    lane_behind = np.block([[cosine, sine], [-sine, cosine]])
    piece = np.arange(radix)
    turn = 2.0 * np.pi * piece[:, None] * (near[None, :] + 0.25) / (blocks * radix)
    turn = np.broadcast_to(turn[:, :, None], (radix, blocks, LANES))
    key = near[None, :] + blocks * piece[:, None] + 0.25
    fine = 2.0 * np.pi * key[:, :, None] * lane[None, None, :] / total
    angles = np.stack([turn, fine])
    twist = np.stack([np.cos(angles), np.sin(angles)], axis=1).astype(np.float32)
    return (
        split_table(ahead, 1),
        split_table(lane_ahead, 0),
        split_table(lane_behind, 0),
        split_table(behind, 1),
        twist,
    )


def halves(values):
    high = values.astype(jnp.bfloat16)
    low = (values - high.astype(jnp.float32)).astype(jnp.bfloat16)
    return high, low


def dot(a, b):
    return jnp.dot(a, b, preferred_element_type=jnp.float32)


def pack_kernel(taps_in, gate_in, value_in, cotangent_in, gate_out_in, out, *scratch):
    sources = (taps_in, gate_in, value_in, cotangent_in, gate_out_in)
    buffers, sems = scratch[:5], scratch[5]
    copies = [pltpu.make_async_copy(src, dst, sems.at[i]) for i, (src, dst) in enumerate(zip(sources, buffers))]
    for copy in copies:
        copy.start()
    radix = taps_in.shape[0] // LANES
    taps, first, value, grad, second = buffers

    def send(s, take):
        for a in range(radix):
            turned = take(slice(a * LANES, (a + 1) * LANES)).T
            at = (a * 3 + s) * SUB
            out[:, at : at + SUB, :] = turned.reshape(-1, SUB, LANES)

    copies[0].wait()
    send(1, lambda r: taps[r, :])
    copies[1].wait()
    copies[2].wait()
    send(0, lambda r: first[r, :].astype(jnp.float32) * value[r, :].astype(jnp.float32))
    copies[3].wait()
    copies[4].wait()
    send(2, lambda r: grad[r, :].astype(jnp.float32) * second[r, :].astype(jnp.float32))


def spectral_kernel(
    data, ahead, lane_ahead, lane_behind, behind, twist, out, xs, fs, gs, spec, gain
):
    blocks = data.shape[0]
    radix = twist.shape[2]
    half_root = math.sqrt(0.75)
    width = radix * LANES
    total = jnp.zeros((SUB, LANES), jnp.float32)
    for s in range(3):
        for a in range(radix):
            at = (a * 3 + s) * SUB
            high, low = halves(data[:, at : at + SUB, :].reshape(blocks * SUB, LANES))
            to = s * width + a * LANES
            for j, v in enumerate((high, low, high)):
                xs[j, :, to : to + LANES] = v
    for a in range(radix):
        mixed = data[:, a * 3 * SUB : a * 3 * SUB + SUB, :]
        up = data[:, (a * 3 + 2) * SUB : (a * 3 + 3) * SUB, :]
        total = total + jnp.sum(mixed * up, axis=0)
    skip_at = 3 * radix * SUB
    out[:, skip_at : skip_at + SUB, :] = jnp.broadcast_to(total[None], (blocks, SUB, LANES))

    stacked = xs[...].reshape(3 * blocks * SUB, 3 * width)
    fs[...] = dot(ahead[...], stacked).reshape(2, SUB, blocks, 3 * width)

    for s in range(3):

        def forward(c, _, s=s):
            real, imag = [], []
            for a in range(radix):
                at = s * width + a * LANES
                re = fs[0, c, :, at : at + LANES]
                im = fs[1, c, :, at : at + LANES]
                if a:
                    co = twist[0, 0, a]
                    si = twist[0, 1, a]
                    re, im = re * co + im * si, im * co - re * si
                real.append(re)
                imag.append(im)
            sum_re, sum_im = real[1] + real[2], imag[1] + imag[2]
            mid_re, mid_im = real[0] - 0.5 * sum_re, imag[0] - 0.5 * sum_im
            dif_re = half_root * (real[1] - real[2])
            dif_im = half_root * (imag[1] - imag[2])
            outs = (
                (real[0] + sum_re, imag[0] + sum_im),
                (mid_re + dif_im, mid_im - dif_re),
                (mid_re - dif_im, mid_im + dif_re),
            )
            for e, (re, im) in enumerate(outs):
                co = twist[1, 0, e]
                si = twist[1, 1, e]
                for p, v in enumerate((re * co + im * si, im * co - re * si)):
                    high, low = halves(v)
                    for j, w in enumerate((high, low, high)):
                        at = (2 * j + p) * LANES
                        gs[s, e, c, :, at : at + LANES] = w
            return 0

        lax.fori_loop(0, SUB, forward, 0, unroll=True)
        rows = radix * SUB * blocks
        result = dot(gs[s].reshape(rows, 6 * LANES), lane_ahead[...])
        spec[s] = result.reshape(radix, SUB, blocks, 2 * LANES)

    def product(c, _):
        for e in range(radix):
            mr, mi = spec[0, e, c, :, :LANES], spec[0, e, c, :, LANES:]
            hr, hi = spec[1, e, c, :, :LANES], spec[1, e, c, :, LANES:]
            ur, ui = spec[2, e, c, :, :LANES], spec[2, e, c, :, LANES:]
            outs = (
                (hr * mr - hi * mi, hr * mi + hi * mr),
                (hr * ur + hi * ui, hr * ui - hi * ur),
                (mr * ur + mi * ui, mr * ui - mi * ur),
            )
            for s, pair in enumerate(outs):
                for p, v in enumerate(pair):
                    high, low = halves(v)
                    for j, w in enumerate((high, low, high)):
                        at = (2 * j + p) * LANES
                        gs[s, e, c, :, at : at + LANES] = w
        return 0

    lax.fori_loop(0, SUB, product, 0, unroll=True)

    for s in range(3):
        rows = radix * SUB * blocks
        result = dot(gs[s].reshape(rows, 6 * LANES), lane_behind[...])
        spec[s] = result.reshape(radix, SUB, blocks, 2 * LANES)

        def backward(c, _, s=s):
            real, imag = [], []
            for e in range(radix):
                re, im = spec[s, e, c, :, :LANES], spec[s, e, c, :, LANES:]
                co = twist[1, 0, e]
                si = twist[1, 1, e]
                real.append(re * co - im * si)
                imag.append(im * co + re * si)
            sum_re, sum_im = real[1] + real[2], imag[1] + imag[2]
            mid_re, mid_im = real[0] - 0.5 * sum_re, imag[0] - 0.5 * sum_im
            dif_re = half_root * (real[1] - real[2])
            dif_im = half_root * (imag[1] - imag[2])
            outs = (
                (real[0] + sum_re, imag[0] + sum_im),
                (mid_re - dif_im, mid_im + dif_re),
                (mid_re + dif_im, mid_im - dif_re),
            )
            for a, (re, im) in enumerate(outs):
                if a:
                    co = twist[0, 0, a]
                    si = twist[0, 1, a]
                    re, im = re * co - im * si, im * co + re * si
                at = s * width + a * LANES
                for p, v in enumerate((re, im)):
                    high, low = halves(v)
                    for j, w in enumerate((high, low, high)):
                        gain[j, p, c, :, at : at + LANES] = w
            return 0

        lax.fori_loop(0, SUB, backward, 0, unroll=True)

    stacked = gain[...].reshape(3 * 2 * SUB * blocks, 3 * width)
    result = dot(behind[...], stacked)
    for s in range(3):
        for a in range(radix):
            at = (a * 3 + s) * SUB
            to = s * width + a * LANES
            out[:, at : at + SUB, :] = result[:, to : to + LANES].reshape(blocks, SUB, LANES)


def unpack_kernel(
    data, gate_in, value_in, gate_out, cotangent, skip_gain, g_in, g_value, g_out, g_taps, g_skip, *, scale
):
    channels = gate_in.shape[1]
    radix = gate_in.shape[0] // LANES
    gain = skip_gain[...]
    for a in range(radix):
        rows = slice(a * LANES, (a + 1) * LANES)
        conv, back, lagged = (
            data[:, (a * 3 + s) * SUB : (a * 3 + s + 1) * SUB, :].reshape(channels, LANES).T
            for s in range(3)
        )
        first = gate_in[rows, :].astype(jnp.float32)
        value = value_in[rows, :].astype(jnp.float32)
        second = gate_out[rows, :].astype(jnp.float32)
        grad = cotangent[rows, :].astype(jnp.float32)
        g_out[rows, :] = (grad * (conv + gain * (first * value))).astype(g_out.dtype)
        mid = back + gain * (grad * second)
        g_in[rows, :] = (mid * value).astype(g_in.dtype)
        g_value[rows, :] = (mid * first).astype(g_value.dtype)
        g_taps[rows, :] = lagged * scale
    at = 3 * radix * SUB
    share = data[:, at : at + SUB, :].reshape(channels, LANES).T
    g_skip[...] = jnp.sum(share, axis=0, keepdims=True) * scale


PARAMS = pltpu.CompilerParams(vmem_limit_bytes=24 * 1024 * 1024)
ON_CHIP = pl.BlockSpec(memory_space=pltpu.VMEM)
IN_HBM = pl.BlockSpec(memory_space=pltpu.HBM)


def held(x):
    return x if INTERPRET else pltpu.with_memory_space_constraint(x, pltpu.HBM)


def call(kernel, out_shape, scratch=(), in_specs=None):
    extra = {} if in_specs is None else {"in_specs": in_specs}
    out_specs = jax.tree.map(lambda _: ON_CHIP, out_shape)
    return pl.pallas_call(
        kernel,
        out_shape=out_shape,
        out_specs=out_specs,
        scratch_shapes=scratch,
        compiler_params=PARAMS,
        interpret=INTERPRET,
        **extra,
    )


def pack(gate_in, value_in, gate_out, cotangent, taps):
    rows, channels = taps.shape
    height = 3 * rows // LANES * SUB
    shape = jax.ShapeDtypeStruct((channels // SUB, height, LANES), jnp.float32)
    operands = tuple(held(x) for x in (taps, gate_in, value_in, cotangent, gate_out))
    scratch = [pltpu.VMEM(x.shape, x.dtype) for x in operands]
    scratch.append(pltpu.SemaphoreType.DMA((len(operands),)))
    return call(pack_kernel, shape, scratch, [IN_HBM] * len(operands))(*operands)


def spectral(data):
    blocks = data.shape[0]
    radix = data.shape[1] // (3 * SUB)
    width = radix * LANES
    consts = [jnp.asarray(t) for t in tables(blocks, radix)]
    shape = jax.ShapeDtypeStruct((blocks, (3 * radix + 1) * SUB, LANES), jnp.float32)
    scratch = [
        pltpu.VMEM((3, blocks * SUB, 3 * width), jnp.bfloat16),
        pltpu.VMEM((2, SUB, blocks, 3 * width), jnp.float32),
        pltpu.VMEM((3, radix, SUB, blocks, 6 * LANES), jnp.bfloat16),
        pltpu.VMEM((3, radix, SUB, blocks, 2 * LANES), jnp.float32),
        pltpu.VMEM((3, 2, SUB, blocks, 3 * width), jnp.bfloat16),
    ]
    return call(spectral_kernel, shape, scratch)(data, *consts)


def unpack(data, gate_in, value_in, gate_out, cotangent, skip_gain, scale):
    rows, channels = gate_in.shape
    half = jax.ShapeDtypeStruct((rows, channels), jnp.bfloat16)
    shapes = (
        half,
        half,
        half,
        jax.ShapeDtypeStruct((rows, channels), jnp.float32),
        jax.ShapeDtypeStruct((1, channels), jnp.float32),
    )

    def kernel(*refs):
        unpack_kernel(*refs, scale=scale)

    outs = call(kernel, shapes)(data, gate_in, value_in, gate_out, cotangent, skip_gain[None])
    return (*outs[:4], outs[4][0])


def body(gate_in, value_in, gate_out, filter_taps, skip_gain, cotangent):
    scale = 1.0 / math.sqrt(lax.axis_size(AXES) * gate_in.shape[0])
    data = pack(gate_in, value_in, gate_out, cotangent, filter_taps)
    data = lax.all_to_all(data, AXES, split_axis=0, concat_axis=0, tiled=True)
    data = spectral(data)
    data = lax.all_to_all(data, AXES, split_axis=0, concat_axis=0, tiled=True)
    return unpack(data, gate_in, value_in, gate_out, cotangent, skip_gain, scale)


def solution(mesh):
    spread = P(AXES, "ch")
    return jax.shard_map(
        body,
        mesh=mesh,
        in_specs=(spread, spread, spread, spread, P("ch"), spread),
        out_specs=(spread, spread, spread, spread, P("ch")),
        check_vma=False,
    )
```

```python
import math

import jax
import jax.numpy as jnp
import numpy as np
from jax import lax
from jax.experimental import pallas as pl
from jax.experimental.pallas import tpu as pltpu
from jax.sharding import PartitionSpec as P

AXES = ("grp", "blk")
LANES = 128
SUB = 8
INTERPRET = False


def split_table(table):
    high = table.astype(jnp.bfloat16)
    low = (table - high.astype(np.float64)).astype(jnp.bfloat16)
    return np.concatenate([high, high, low], axis=0)


NEAR, FAR = 4, 8


def tables(blocks, radix):
    total = blocks * radix * LANES
    lane = np.arange(LANES)
    inner = 2.0 * np.pi * np.outer(lane, lane) / LANES
    cosine, sine = np.cos(inner), np.sin(inner)
    lane_ahead = np.block([[cosine, -sine], [sine, cosine]])
    lane_behind = np.block([[cosine, sine], [-sine, cosine]])
    far, near, piece = np.meshgrid(np.arange(FAR), np.arange(NEAR), np.arange(radix), indexing="ij")
    span = blocks * radix
    from_piece = blocks * pow(blocks, -1, radix) * pow(radix - 1, -1, radix)
    from_block = radix * pow(radix, -1, blocks) * radix
    key = (from_piece * piece + from_block * (far + FAR * near)) % span
    fine = 2.0 * np.pi * (key.reshape(-1, 1) + 0.25) * lane / total
    twist = np.stack([np.cos(fine), np.sin(fine)]).astype(np.float32)
    twist = np.repeat(twist[:, :, None, :], SUB, axis=2)
    return split_table(lane_ahead), split_table(lane_behind), twist


def halves(values):
    high = values.astype(jnp.bfloat16)
    low = (values - high.astype(jnp.float32)).astype(jnp.bfloat16)
    return high, low


def dot(a, b):
    return jnp.dot(a, b, preferred_element_type=jnp.float32)


def turn(pair, angle):
    re, im = pair
    eighth = round(angle * 8) % 8
    if abs(angle * 8 - round(angle * 8)) < 1e-9:
        if eighth == 0:
            return re, im
        if eighth == 2:
            return -im, re
        if eighth == 4:
            return -re, -im
        if eighth == 6:
            return im, -re
        root = math.sqrt(0.5)
        if eighth == 1:
            return root * (re - im), root * (re + im)
        if eighth == 3:
            return -root * (re + im), root * (re - im)
        if eighth == 5:
            return root * (im - re), -root * (re + im)
        return root * (re + im), root * (im - re)
    c, s = math.cos(2.0 * math.pi * angle), math.sin(2.0 * math.pi * angle)
    return c * re - s * im, c * im + s * re


def plus(x, y):
    return x[0] + y[0], x[1] + y[1]


def minus(x, y):
    return x[0] - y[0], x[1] - y[1]


def plus_i(x, y, sign):
    if sign > 0:
        return x[0] - y[1], x[1] + y[0]
    return x[0] + y[1], x[1] - y[0]


def four(x, sign):
    p, m = plus(x[0], x[2]), minus(x[0], x[2])
    q, n = plus(x[1], x[3]), minus(x[1], x[3])
    return [plus(p, q), plus_i(m, n, sign), minus(p, q), plus_i(m, n, -sign)]


def eight(x, sign):
    even, odd = four(x[0::2], sign), four(x[1::2], sign)
    odd = [odd[0]] + [turn(odd[k], sign * k / 8) for k in (1, 2, 3)]
    return [plus(even[k], odd[k]) for k in range(4)] + [minus(even[k], odd[k]) for k in range(4)]


def three(x, sign):
    total, gap = plus(x[1], x[2]), minus(x[1], x[2])
    half_root = math.sqrt(0.75)
    mid = x[0][0] - 0.5 * total[0], x[0][1] - 0.5 * total[1]
    gap = half_root * gap[0], half_root * gap[1]
    return [plus(x[0], total), plus_i(mid, gap, sign), plus_i(mid, gap, -sign)]


def pack_kernel(taps_in, gate_in, value_in, cotangent_in, gate_out_in, out, *scratch):
    sources = (taps_in, gate_in, value_in, cotangent_in, gate_out_in)
    buffers, sems = scratch[:5], scratch[5]
    copies = [pltpu.make_async_copy(src, dst, sems.at[i]) for i, (src, dst) in enumerate(zip(sources, buffers))]
    for copy in copies:
        copy.start()
    radix = taps_in.shape[0] // LANES
    taps, first, value, grad, second = buffers

    def send(s, take):
        for a in range(radix):
            turned = take(slice(a * LANES, (a + 1) * LANES)).T
            at = (a * 3 + s) * SUB
            out[:, at : at + SUB, :] = turned.reshape(-1, SUB, LANES)

    copies[0].wait()
    send(1, lambda r: taps[r, :])
    copies[1].wait()
    copies[2].wait()
    send(0, lambda r: first[r, :].astype(jnp.float32) * value[r, :].astype(jnp.float32))
    copies[3].wait()
    copies[4].wait()
    send(2, lambda r: grad[r, :].astype(jnp.float32) * second[r, :].astype(jnp.float32))


def spectral_kernel(data, lane_ahead, lane_behind, twist, out, ts, gs, spec):
    blocks = data.shape[0]
    radix = data.shape[1] // (3 * SUB)
    span = blocks * radix
    scale = 1.0 / (span * LANES)
    height = 3 * radix * SUB + 1
    rows = span * SUB

    def at(a, s):
        return slice((a * 3 + s) * SUB, (a * 3 + s + 1) * SUB)

    total = jnp.zeros((SUB, LANES), jnp.float32)
    for a in range(radix):
        total = total + jnp.sum(data[:, at(a, 0), :] * data[:, at(a, 2), :], axis=0)
    share = jnp.concatenate([jnp.sum(total.T, axis=0, keepdims=True)] * (LANES // SUB), axis=1)
    for d in range(blocks):
        out[d * height + height - 1 : (d + 1) * height, :] = share

    def store(s, row, pairs):
        for p in range(2):
            high, low = halves(jnp.concatenate([pair[p] for pair in pairs], axis=0))
            for j, w in enumerate((high, low, high)):
                lanes = (2 * j + p) * LANES
                gs[s, row : row + 2 * SUB, lanes : lanes + LANES] = w

    def forward(s):
        for a in range(radix):
            for n0 in range(NEAR):
                values = []
                for n1 in range(FAR):
                    m = NEAR * n1 + n0
                    d = ((m - a) * pow(radix, -1, blocks)) % blocks
                    x = data[d, at(a, s), :]
                    angle = 2.0 * math.pi * (radix * d + a) / (4 * span)
                    values.append((math.cos(angle) * x, -math.sin(angle) * x))
                for k1, pair in enumerate(eight(values, -1)):
                    re, im = turn(pair, -n0 * k1 / blocks)
                    ts[s, a, n0, k1, 0] = re
                    ts[s, a, n0, k1, 1] = im
        for k1 in range(FAR):
            quads = [
                four([(ts[s, a, n0, k1, 0], ts[s, a, n0, k1, 1]) for n0 in range(NEAR)], -1)
                for a in range(radix)
            ]
            for k2 in range(0, NEAR, 2):
                pairs = []
                for k in (k2, k2 + 1):
                    group = []
                    for e, (re, im) in enumerate(three([quads[a][k] for a in range(radix)], -1)):
                        row = (k1 * NEAR + k) * radix + e
                        co, si = twist[0, row], twist[1, row]
                        group.append((re * co + im * si, im * co - re * si))
                    pairs.append(group)
                for e in range(radix):
                    row = (e * blocks + k1 * NEAR + k2) * SUB
                    store(s, row, [pairs[0][e], pairs[1][e]])
        spec[s] = dot(gs[s], lane_ahead[...])

    def product(s):
        left, right = ((1, 0), (1, 2), (0, 2))[s]
        for row in range(0, rows, 2 * SUB):
            lr, li = spec[left, row : row + 2 * SUB, :LANES], spec[left, row : row + 2 * SUB, LANES:]
            rr, ri = spec[right, row : row + 2 * SUB, :LANES], spec[right, row : row + 2 * SUB, LANES:]
            if s == 0:
                both = lr * rr - li * ri, lr * ri + li * rr
            else:
                both = lr * rr + li * ri, lr * ri - li * rr
            for p in range(2):
                high, low = halves(both[p])
                for j, w in enumerate((high, low, high)):
                    lanes = (2 * j + p) * LANES
                    gs[3 + s, row : row + 2 * SUB, lanes : lanes + LANES] = w
        spec[3 + s] = dot(gs[3 + s], lane_behind[...])

    def backward(s):
        for k1 in range(FAR):
            quads = []
            for k2 in range(NEAR):
                trio = []
                for e in range(radix):
                    row = (e * blocks + k1 * NEAR + k2) * SUB
                    re, im = spec[3 + s, row : row + SUB, :LANES], spec[3 + s, row : row + SUB, LANES:]
                    row = (k1 * NEAR + k2) * radix + e
                    co, si = twist[0, row], twist[1, row]
                    trio.append((re * co - im * si, im * co + re * si))
                quads.append(three(trio, 1))
            for a in range(radix):
                for n0, pair in enumerate(four([quads[k2][a] for k2 in range(NEAR)], 1)):
                    re, im = turn(pair, n0 * k1 / blocks)
                    ts[s, a, n0, k1, 0] = re
                    ts[s, a, n0, k1, 1] = im
        for a in range(radix):
            for n0 in range(NEAR):
                values = eight([(ts[s, a, n0, k1, 0], ts[s, a, n0, k1, 1]) for k1 in range(FAR)], 1)
                for n1, (re, im) in enumerate(values):
                    m = NEAR * n1 + n0
                    d = ((m - a) * pow(radix, -1, blocks)) % blocks
                    angle = 2.0 * math.pi * (radix * d + a) / (4 * span)
                    row = d * height + (a * 3 + s) * SUB
                    out[row : row + SUB, :] = (scale * math.cos(angle)) * re - (scale * math.sin(angle)) * im

    forward(0)
    forward(1)
    product(0)
    forward(2)
    backward(0)
    product(1)
    product(2)
    backward(1)
    backward(2)


def unpack_kernel(
    data, gate_in, value_in, gate_out, cotangent, skip_gain, g_in, g_value, g_out, g_taps, g_skip, *, scale
):
    channels = gate_in.shape[1]
    radix = gate_in.shape[0] // LANES
    gain = skip_gain[...]
    height = 3 * radix * SUB + 1

    def piece(a, s):
        at = (a * 3 + s) * SUB
        tiles = [data[d * height + at : d * height + at + SUB, :] for d in range(channels // SUB)]
        return jnp.concatenate(tiles, axis=0).T

    for a in range(radix):
        rows = slice(a * LANES, (a + 1) * LANES)
        conv, back, lagged = (piece(a, s) for s in range(3))
        first = gate_in[rows, :].astype(jnp.float32)
        value = value_in[rows, :].astype(jnp.float32)
        second = gate_out[rows, :].astype(jnp.float32)
        grad = cotangent[rows, :].astype(jnp.float32)
        g_out[rows, :] = (grad * (conv + gain * (first * value))).astype(g_out.dtype)
        mid = back + gain * (grad * second)
        g_in[rows, :] = (mid * value).astype(g_in.dtype)
        g_value[rows, :] = (mid * first).astype(g_value.dtype)
        g_taps[rows, :] = lagged * scale
    for d in range(channels // SUB):
        share = data[(d + 1) * height - 1 : (d + 1) * height, :SUB]
        g_skip[:, d * SUB : (d + 1) * SUB] = share * scale


PARAMS = pltpu.CompilerParams(vmem_limit_bytes=24 * 1024 * 1024)
ON_CHIP = pl.BlockSpec(memory_space=pltpu.VMEM)
IN_HBM = pl.BlockSpec(memory_space=pltpu.HBM)


def held(x):
    return x if INTERPRET else pltpu.with_memory_space_constraint(x, pltpu.HBM)


def call(kernel, out_shape, scratch=(), in_specs=None):
    extra = {} if in_specs is None else {"in_specs": in_specs}
    out_specs = jax.tree.map(lambda _: ON_CHIP, out_shape)
    return pl.pallas_call(
        kernel,
        out_shape=out_shape,
        out_specs=out_specs,
        scratch_shapes=scratch,
        compiler_params=PARAMS,
        interpret=INTERPRET,
        **extra,
    )


def pack(gate_in, value_in, gate_out, cotangent, taps):
    rows, channels = taps.shape
    height = 3 * rows // LANES * SUB
    shape = jax.ShapeDtypeStruct((channels // SUB, height, LANES), jnp.float32)
    operands = tuple(held(x) for x in (taps, gate_in, value_in, cotangent, gate_out))
    scratch = [pltpu.VMEM(x.shape, x.dtype) for x in operands]
    scratch.append(pltpu.SemaphoreType.DMA((len(operands),)))
    return call(pack_kernel, shape, scratch, [IN_HBM] * len(operands))(*operands)


def spectral(data):
    blocks = data.shape[0]
    radix = data.shape[1] // (3 * SUB)
    consts = [jnp.asarray(t) for t in tables(blocks, radix)]
    shape = jax.ShapeDtypeStruct((blocks * (3 * radix * SUB + 1), LANES), jnp.float32)
    rows = blocks * radix * SUB
    scratch = [
        pltpu.VMEM((3, radix, NEAR, FAR, 2, SUB, LANES), jnp.float32),
        pltpu.VMEM((6, rows, 6 * LANES), jnp.bfloat16),
        pltpu.VMEM((6, rows, 2 * LANES), jnp.float32),
    ]
    return call(spectral_kernel, shape, scratch)(data, *consts)


def unpack(data, gate_in, value_in, gate_out, cotangent, skip_gain, scale):
    rows, channels = gate_in.shape
    half = jax.ShapeDtypeStruct((rows, channels), jnp.bfloat16)
    shapes = (
        half,
        half,
        half,
        jax.ShapeDtypeStruct((rows, channels), jnp.float32),
        jax.ShapeDtypeStruct((1, channels), jnp.float32),
    )

    def kernel(*refs):
        unpack_kernel(*refs, scale=scale)

    outs = call(kernel, shapes)(data, gate_in, value_in, gate_out, cotangent, skip_gain[None])
    return (*outs[:4], outs[4][0])


def body(gate_in, value_in, gate_out, filter_taps, skip_gain, cotangent):
    scale = 1.0 / math.sqrt(lax.axis_size(AXES) * gate_in.shape[0])
    data = pack(gate_in, value_in, gate_out, cotangent, filter_taps)
    data = lax.all_to_all(data, AXES, split_axis=0, concat_axis=0, tiled=True)
    data = spectral(data)
    rows = data.reshape(lax.axis_size(AXES), -1, 1, LANES)
    data = lax.all_to_all(rows, AXES, split_axis=0, concat_axis=0, tiled=True).reshape(data.shape)
    return unpack(data, gate_in, value_in, gate_out, cotangent, skip_gain, scale)


def solution(mesh):
    spread = P(AXES, "ch")
    return jax.shard_map(
        body,
        mesh=mesh,
        in_specs=(spread, spread, spread, spread, P("ch"), spread),
        out_specs=(spread, spread, spread, spread, P("ch")),
        check_vma=False,
    )
```

```python
import math

import jax
import jax.numpy as jnp
import numpy as np
from jax import lax
from jax.experimental import pallas as pl
from jax.experimental.pallas import tpu as pltpu
from jax.sharding import PartitionSpec as P

AXES = ("grp", "blk")
LANES = 128
SUB = 8
INTERPRET = False


def split_table(table):
    high = table.astype(jnp.bfloat16)
    low = (table - high.astype(np.float64)).astype(jnp.bfloat16)
    return np.concatenate([high, high, low], axis=0)


NEAR, FAR = 4, 8


def tables(blocks, radix):
    total = blocks * radix * LANES
    lane = np.arange(LANES)
    inner = 2.0 * np.pi * np.outer(lane, lane) / LANES
    cosine, sine = np.cos(inner), np.sin(inner)
    lane_ahead = np.block([[cosine, -sine], [sine, cosine]])
    lane_behind = np.block([[cosine, sine], [-sine, cosine]])
    far, near, piece = np.meshgrid(np.arange(FAR), np.arange(NEAR), np.arange(radix), indexing="ij")
    span = blocks * radix
    from_piece = blocks * pow(blocks, -1, radix) * pow(radix - 1, -1, radix)
    from_block = radix * pow(radix, -1, blocks) * radix
    key = (from_piece * piece + from_block * (far + FAR * near)) % span
    fine = 2.0 * np.pi * (key.reshape(-1, 1) + 0.25) * lane / total
    twist = np.stack([np.cos(fine), np.sin(fine)]).astype(np.float32)
    twist = np.repeat(twist[:, :, None, :], SUB, axis=2)
    return split_table(lane_ahead), split_table(lane_behind), twist


def halves(values):
    high = values.astype(jnp.bfloat16)
    low = (values - high.astype(jnp.float32)).astype(jnp.bfloat16)
    return high, low


def dot(a, b):
    return jnp.dot(a, b, preferred_element_type=jnp.float32)


def turn(pair, angle):
    re, im = pair
    eighth = round(angle * 8) % 8
    if abs(angle * 8 - round(angle * 8)) < 1e-9:
        if eighth == 0:
            return re, im
        if eighth == 2:
            return -im, re
        if eighth == 4:
            return -re, -im
        if eighth == 6:
            return im, -re
        root = math.sqrt(0.5)
        if eighth == 1:
            return root * (re - im), root * (re + im)
        if eighth == 3:
            return -root * (re + im), root * (re - im)
        if eighth == 5:
            return root * (im - re), -root * (re + im)
        return root * (re + im), root * (im - re)
    c, s = math.cos(2.0 * math.pi * angle), math.sin(2.0 * math.pi * angle)
    return c * re - s * im, c * im + s * re


def plus(x, y):
    return x[0] + y[0], x[1] + y[1]


def minus(x, y):
    return x[0] - y[0], x[1] - y[1]


def plus_i(x, y, sign):
    if sign > 0:
        return x[0] - y[1], x[1] + y[0]
    return x[0] + y[1], x[1] - y[0]


def four(x, sign):
    p, m = plus(x[0], x[2]), minus(x[0], x[2])
    q, n = plus(x[1], x[3]), minus(x[1], x[3])
    return [plus(p, q), plus_i(m, n, sign), minus(p, q), plus_i(m, n, -sign)]


def eight(x, sign):
    even, odd = four(x[0::2], sign), four(x[1::2], sign)
    odd = [odd[0]] + [turn(odd[k], sign * k / 8) for k in (1, 2, 3)]
    return [plus(even[k], odd[k]) for k in range(4)] + [minus(even[k], odd[k]) for k in range(4)]


def three(x, sign):
    total, gap = plus(x[1], x[2]), minus(x[1], x[2])
    half_root = math.sqrt(0.75)
    mid = x[0][0] - 0.5 * total[0], x[0][1] - 0.5 * total[1]
    gap = half_root * gap[0], half_root * gap[1]
    return [plus(x[0], total), plus_i(mid, gap, sign), plus_i(mid, gap, -sign)]


def pack_kernel(taps_in, gate_in, value_in, cotangent_in, gate_out_in, out, *scratch):
    sources = (taps_in, gate_in, value_in, cotangent_in, gate_out_in)
    buffers, sems = scratch[:5], scratch[5]
    copies = [pltpu.make_async_copy(src, dst, sems.at[i]) for i, (src, dst) in enumerate(zip(sources, buffers))]
    for copy in copies:
        copy.start()
    radix = taps_in.shape[0] // LANES
    taps, first, value, grad, second = buffers

    def send(s, take):
        for a in range(radix):
            turned = take(slice(a * LANES, (a + 1) * LANES)).T
            at = (a * 3 + s) * SUB
            out[:, at : at + SUB, :] = turned.reshape(-1, SUB, LANES)

    copies[0].wait()
    send(1, lambda r: taps[r, :])
    copies[1].wait()
    copies[2].wait()
    send(0, lambda r: first[r, :].astype(jnp.float32) * value[r, :].astype(jnp.float32))
    copies[3].wait()
    copies[4].wait()
    send(2, lambda r: grad[r, :].astype(jnp.float32) * second[r, :].astype(jnp.float32))


def spectral_kernel(data, lane_ahead, lane_behind, twist, out, ts, gs, spec):
    blocks = data.shape[0]
    radix = data.shape[1] // (3 * SUB)
    span = blocks * radix
    scale = 1.0 / (span * LANES)
    height = 3 * radix * SUB + 1
    rows = span * SUB

    def at(a, s):
        return slice((a * 3 + s) * SUB, (a * 3 + s + 1) * SUB)

    total = jnp.zeros((SUB, LANES), jnp.float32)
    for a in range(radix):
        total = total + jnp.sum(data[:, at(a, 0), :] * data[:, at(a, 2), :], axis=0)
    share = jnp.concatenate([jnp.sum(total.T, axis=0, keepdims=True)] * (LANES // SUB), axis=1)
    for d in range(blocks):
        out[d * height + height - 1 : (d + 1) * height, :] = share

    def store(s, row, pairs):
        for p in range(2):
            high, low = halves(jnp.concatenate([pair[p] for pair in pairs], axis=0))
            for j, w in enumerate((high, low)):
                lanes = (2 * j + p) * LANES
                gs[s, row : row + 2 * SUB, lanes : lanes + LANES] = w

    def forward(s):
        for a in range(radix):
            for n0 in range(NEAR):
                values = []
                for n1 in range(FAR):
                    m = NEAR * n1 + n0
                    d = ((m - a) * pow(radix, -1, blocks)) % blocks
                    x = data[d, at(a, s), :]
                    angle = 2.0 * math.pi * (radix * d + a) / (4 * span)
                    values.append((math.cos(angle) * x, -math.sin(angle) * x))
                for k1, pair in enumerate(eight(values, -1)):
                    re, im = turn(pair, -n0 * k1 / blocks)
                    ts[s, a, n0, k1, 0] = re
                    ts[s, a, n0, k1, 1] = im
                yield
        for k1 in range(FAR):
            quads = [
                four([(ts[s, a, n0, k1, 0], ts[s, a, n0, k1, 1]) for n0 in range(NEAR)], -1)
                for a in range(radix)
            ]
            for k2 in range(0, NEAR, 2):
                pairs = []
                for k in (k2, k2 + 1):
                    group = []
                    for e, (re, im) in enumerate(three([quads[a][k] for a in range(radix)], -1)):
                        row = (k1 * NEAR + k) * radix + e
                        co, si = twist[0, row], twist[1, row]
                        group.append((re * co + im * si, im * co - re * si))
                    pairs.append(group)
                for e in range(radix):
                    row = (e * blocks + k1 * NEAR + k2) * SUB
                    store(s, row, [pairs[0][e], pairs[1][e]])
            yield

    def product(s):
        left, right = ((1, 0), (1, 2), (0, 2))[s]
        for row in range(0, rows, 2 * SUB):
            lr, li = spec[left, row : row + 2 * SUB, :LANES], spec[left, row : row + 2 * SUB, LANES:]
            rr, ri = spec[right, row : row + 2 * SUB, :LANES], spec[right, row : row + 2 * SUB, LANES:]
            if s == 0:
                both = lr * rr - li * ri, lr * ri + li * rr
            else:
                both = lr * rr + li * ri, lr * ri - li * rr
            for p in range(2):
                high, low = halves(both[p])
                for j, w in enumerate((high, low)):
                    lanes = (2 * j + p) * LANES
                    gs[3 + s, row : row + 2 * SUB, lanes : lanes + LANES] = w
            if row % (6 * SUB) == 0:
                yield

    def backward(s):
        for k1 in range(FAR):
            quads = []
            for k2 in range(NEAR):
                trio = []
                for e in range(radix):
                    row = (e * blocks + k1 * NEAR + k2) * SUB
                    re, im = spec[3 + s, row : row + SUB, :LANES], spec[3 + s, row : row + SUB, LANES:]
                    row = (k1 * NEAR + k2) * radix + e
                    co, si = twist[0, row], twist[1, row]
                    trio.append((re * co - im * si, im * co + re * si))
                quads.append(three(trio, 1))
            for a in range(radix):
                for n0, pair in enumerate(four([quads[k2][a] for k2 in range(NEAR)], 1)):
                    re, im = turn(pair, n0 * k1 / blocks)
                    ts[s, a, n0, k1, 0] = re
                    ts[s, a, n0, k1, 1] = im
            yield
        for a in range(radix):
            for n0 in range(NEAR):
                values = eight([(ts[s, a, n0, k1, 0], ts[s, a, n0, k1, 1]) for k1 in range(FAR)], 1)
                for n1, (re, im) in enumerate(values):
                    m = NEAR * n1 + n0
                    d = ((m - a) * pow(radix, -1, blocks)) % blocks
                    angle = 2.0 * math.pi * (radix * d + a) / (4 * span)
                    row = d * height + (a * 3 + s) * SUB
                    out[row : row + SUB, :] = (scale * math.cos(angle)) * re - (scale * math.sin(angle)) * im
                yield

    def lane_dots(s, table):
        step = rows // 3
        for row in range(0, rows, step):
            left = gs[s, row : row + step]
            main = dot(left, table[: 4 * LANES])
            spec[s, row : row + step] = main + dot(left[:, : 2 * LANES], table[4 * LANES :])
            yield

    def mix(vector, *dots):
        gap = max(1, 18 // max(1, 3 * len(dots)))
        chain = (piece for step in dots for piece in step)
        for count, _ in enumerate(vector):
            if count % gap == 0:
                next(chain, None)
        for _ in chain:
            pass

    mix(forward(0))
    mix(forward(1), lane_dots(0, lane_ahead))
    mix(forward(2), lane_dots(1, lane_ahead))
    mix(product(0), lane_dots(2, lane_ahead))
    mix(product(1), lane_dots(3, lane_behind))
    mix(product(2), lane_dots(4, lane_behind))
    mix(backward(0), lane_dots(5, lane_behind))
    mix(backward(1))
    mix(backward(2))


def unpack_kernel(
    data, gate_in, value_in, gate_out, cotangent, skip_gain, g_in, g_value, g_out, g_taps, g_skip, *, scale
):
    channels = gate_in.shape[1]
    radix = gate_in.shape[0] // LANES
    gain = skip_gain[...]
    height = 3 * radix * SUB + 1

    def piece(a, s):
        at = (a * 3 + s) * SUB
        tiles = [data[d * height + at : d * height + at + SUB, :] for d in range(channels // SUB)]
        return jnp.concatenate(tiles, axis=0).T

    for a in range(radix):
        rows = slice(a * LANES, (a + 1) * LANES)
        conv, back, lagged = (piece(a, s) for s in range(3))
        first = gate_in[rows, :].astype(jnp.float32)
        value = value_in[rows, :].astype(jnp.float32)
        second = gate_out[rows, :].astype(jnp.float32)
        grad = cotangent[rows, :].astype(jnp.float32)
        g_out[rows, :] = (grad * (conv + gain * (first * value))).astype(g_out.dtype)
        mid = back + gain * (grad * second)
        g_in[rows, :] = (mid * value).astype(g_in.dtype)
        g_value[rows, :] = (mid * first).astype(g_value.dtype)
        g_taps[rows, :] = lagged * scale
    for d in range(channels // SUB):
        share = data[(d + 1) * height - 1 : (d + 1) * height, :SUB]
        g_skip[:, d * SUB : (d + 1) * SUB] = share * scale


PARAMS = pltpu.CompilerParams(vmem_limit_bytes=24 * 1024 * 1024)
ON_CHIP = pl.BlockSpec(memory_space=pltpu.VMEM)
IN_HBM = pl.BlockSpec(memory_space=pltpu.HBM)


def held(x):
    return x if INTERPRET else pltpu.with_memory_space_constraint(x, pltpu.HBM)


def call(kernel, out_shape, scratch=(), in_specs=None):
    extra = {} if in_specs is None else {"in_specs": in_specs}
    out_specs = jax.tree.map(lambda _: ON_CHIP, out_shape)
    return pl.pallas_call(
        kernel,
        out_shape=out_shape,
        out_specs=out_specs,
        scratch_shapes=scratch,
        compiler_params=PARAMS,
        interpret=INTERPRET,
        **extra,
    )


def pack(gate_in, value_in, gate_out, cotangent, taps):
    rows, channels = taps.shape
    height = 3 * rows // LANES * SUB
    shape = jax.ShapeDtypeStruct((channels // SUB, height, LANES), jnp.float32)
    operands = tuple(held(x) for x in (taps, gate_in, value_in, cotangent, gate_out))
    scratch = [pltpu.VMEM(x.shape, x.dtype) for x in operands]
    scratch.append(pltpu.SemaphoreType.DMA((len(operands),)))
    return call(pack_kernel, shape, scratch, [IN_HBM] * len(operands))(*operands)


def spectral(data):
    blocks = data.shape[0]
    radix = data.shape[1] // (3 * SUB)
    consts = [jnp.asarray(t) for t in tables(blocks, radix)]
    shape = jax.ShapeDtypeStruct((blocks * (3 * radix * SUB + 1), LANES), jnp.float32)
    rows = blocks * radix * SUB
    scratch = [
        pltpu.VMEM((3, radix, NEAR, FAR, 2, SUB, LANES), jnp.float32),
        pltpu.VMEM((6, rows, 4 * LANES), jnp.bfloat16),
        pltpu.VMEM((6, rows, 2 * LANES), jnp.float32),
    ]
    return call(spectral_kernel, shape, scratch)(data, *consts)


def unpack(data, gate_in, value_in, gate_out, cotangent, skip_gain, scale):
    rows, channels = gate_in.shape
    half = jax.ShapeDtypeStruct((rows, channels), jnp.bfloat16)
    shapes = (
        half,
        half,
        half,
        jax.ShapeDtypeStruct((rows, channels), jnp.float32),
        jax.ShapeDtypeStruct((1, channels), jnp.float32),
    )

    def kernel(*refs):
        unpack_kernel(*refs, scale=scale)

    outs = call(kernel, shapes)(data, gate_in, value_in, gate_out, cotangent, skip_gain[None])
    return (*outs[:4], outs[4][0])


def body(gate_in, value_in, gate_out, filter_taps, skip_gain, cotangent):
    scale = 1.0 / math.sqrt(lax.axis_size(AXES) * gate_in.shape[0])
    data = pack(gate_in, value_in, gate_out, cotangent, filter_taps)
    data = lax.all_to_all(data, AXES, split_axis=0, concat_axis=0, tiled=True)
    data = spectral(data)
    rows = data.reshape(lax.axis_size(AXES), -1, 1, LANES)
    data = lax.all_to_all(rows, AXES, split_axis=0, concat_axis=0, tiled=True).reshape(data.shape)
    return unpack(data, gate_in, value_in, gate_out, cotangent, skip_gain, scale)


def solution(mesh):
    spread = P(AXES, "ch")
    return jax.shard_map(
        body,
        mesh=mesh,
        in_specs=(spread, spread, spread, spread, P("ch"), spread),
        out_specs=(spread, spread, spread, spread, P("ch")),
        check_vma=False,
    )
```

```python
import math

import jax
import jax.numpy as jnp
import numpy as np
from jax import lax
from jax.experimental import pallas as pl
from jax.experimental.pallas import tpu as pltpu
from jax.sharding import PartitionSpec as P

PLACE = ("grp", "far", "near")
AXES = ("grp", "near", "far")
LANES = 128
SUB = 8
INTERPRET = False


def split_table(table):
    high = table.astype(jnp.bfloat16)
    low = (table - high.astype(np.float64)).astype(jnp.bfloat16)
    return np.concatenate([high, high, low], axis=0)


NEAR, FAR = 4, 8


def tables(blocks, radix):
    total = blocks * radix * LANES
    lane = np.arange(LANES)
    inner = 2.0 * np.pi * np.outer(lane, lane) / LANES
    cosine, sine = np.cos(inner), np.sin(inner)
    lane_ahead = np.block([[cosine, -sine], [sine, cosine]])
    lane_behind = np.block([[cosine, sine], [-sine, cosine]])
    far, near, piece = np.meshgrid(np.arange(FAR), np.arange(NEAR), np.arange(radix), indexing="ij")
    span = blocks * radix
    from_piece = blocks * pow(blocks, -1, radix) * pow(radix - 1, -1, radix)
    from_block = radix * pow(radix, -1, blocks) * radix
    key = (from_piece * piece + from_block * (far + FAR * near)) % span
    fine = 2.0 * np.pi * (key.reshape(-1, 1) + 0.25) * lane / total
    twist = np.stack([np.cos(fine), np.sin(fine)]).astype(np.float32)
    twist = np.repeat(twist[:, :, None, :], SUB, axis=2)
    return split_table(lane_ahead), split_table(lane_behind), twist


def halves(values):
    high = values.astype(jnp.bfloat16)
    low = (values - high.astype(jnp.float32)).astype(jnp.bfloat16)
    return high, low


def dot(a, b):
    return jnp.dot(a, b, preferred_element_type=jnp.float32)


def turn(pair, angle):
    re, im = pair
    eighth = round(angle * 8) % 8
    if abs(angle * 8 - round(angle * 8)) < 1e-9:
        if eighth == 0:
            return re, im
        if eighth == 2:
            return -im, re
        if eighth == 4:
            return -re, -im
        if eighth == 6:
            return im, -re
        root = math.sqrt(0.5)
        if eighth == 1:
            return root * (re - im), root * (re + im)
        if eighth == 3:
            return -root * (re + im), root * (re - im)
        if eighth == 5:
            return root * (im - re), -root * (re + im)
        return root * (re + im), root * (im - re)
    c, s = math.cos(2.0 * math.pi * angle), math.sin(2.0 * math.pi * angle)
    return c * re - s * im, c * im + s * re


def plus(x, y):
    return x[0] + y[0], x[1] + y[1]


def minus(x, y):
    return x[0] - y[0], x[1] - y[1]


def plus_i(x, y, sign):
    if sign > 0:
        return x[0] - y[1], x[1] + y[0]
    return x[0] + y[1], x[1] - y[0]


def four(x, sign):
    p, m = plus(x[0], x[2]), minus(x[0], x[2])
    q, n = plus(x[1], x[3]), minus(x[1], x[3])
    return [plus(p, q), plus_i(m, n, sign), minus(p, q), plus_i(m, n, -sign)]


def eight(x, sign):
    even, odd = four(x[0::2], sign), four(x[1::2], sign)
    odd = [odd[0]] + [turn(odd[k], sign * k / 8) for k in (1, 2, 3)]
    return [plus(even[k], odd[k]) for k in range(4)] + [minus(even[k], odd[k]) for k in range(4)]


def three(x, sign):
    total, gap = plus(x[1], x[2]), minus(x[1], x[2])
    half_root = math.sqrt(0.75)
    mid = x[0][0] - 0.5 * total[0], x[0][1] - 0.5 * total[1]
    gap = half_root * gap[0], half_root * gap[1]
    return [plus(x[0], total), plus_i(mid, gap, sign), plus_i(mid, gap, -sign)]


def pack_kernel(taps_in, gate_in, value_in, cotangent_in, gate_out_in, out, *scratch):
    sources = (taps_in, gate_in, value_in, cotangent_in, gate_out_in)
    buffers, sems = scratch[:5], scratch[5]
    copies = [pltpu.make_async_copy(src, dst, sems.at[i]) for i, (src, dst) in enumerate(zip(sources, buffers))]
    for copy in copies:
        copy.start()
    radix = taps_in.shape[0] // LANES
    taps, first, value, grad, second = buffers

    def send(s, take):
        for a in range(radix):
            turned = take(slice(a * LANES, (a + 1) * LANES)).T
            at = (a * 3 + s) * SUB
            out[:, at : at + SUB, :] = turned.reshape(-1, SUB, LANES)

    copies[0].wait()
    send(1, lambda r: taps[r, :])
    copies[1].wait()
    copies[2].wait()
    send(0, lambda r: first[r, :].astype(jnp.float32) * value[r, :].astype(jnp.float32))
    copies[3].wait()
    copies[4].wait()
    send(2, lambda r: grad[r, :].astype(jnp.float32) * second[r, :].astype(jnp.float32))


def spectral_kernel(data, lane_ahead, lane_behind, twist, out, ts, gs, spec, *, slots):
    blocks = data.shape[0]
    radix = data.shape[1] // (3 * SUB)
    span = blocks * radix
    scale = 1.0 / (span * LANES)
    height = 3 * radix * SUB + 1
    rows = span * SUB

    def at(a, s):
        return slice((a * 3 + s) * SUB, (a * 3 + s + 1) * SUB)

    total = jnp.zeros((SUB, LANES), jnp.float32)
    for a in range(radix):
        total = total + jnp.sum(data[:, at(a, 0), :] * data[:, at(a, 2), :], axis=0)
    share = jnp.concatenate([jnp.sum(total.T, axis=0, keepdims=True)] * (LANES // SUB), axis=1)
    for d in range(blocks):
        out[d * height + height - 1 : (d + 1) * height, :] = share

    def store(s, row, pairs):
        for p in range(2):
            high, low = halves(jnp.concatenate([pair[p] for pair in pairs], axis=0))
            for j, w in enumerate((high, low)):
                lanes = (2 * j + p) * LANES
                gs[s, row : row + 2 * SUB, lanes : lanes + LANES] = w

    def forward(s):
        for a in range(radix):
            for n0 in range(NEAR):
                values = []
                for n1 in range(FAR):
                    m = NEAR * n1 + n0
                    d = ((m - a) * pow(radix, -1, blocks)) % blocks
                    x = data[slots[d], at(a, s), :]
                    angle = 2.0 * math.pi * (radix * d + a) / (4 * span)
                    values.append((math.cos(angle) * x, -math.sin(angle) * x))
                for k1, pair in enumerate(eight(values, -1)):
                    re, im = turn(pair, -n0 * k1 / blocks)
                    ts[s, a, n0, k1, 0] = re
                    ts[s, a, n0, k1, 1] = im
                yield
        for k1 in range(FAR):
            quads = [
                four([(ts[s, a, n0, k1, 0], ts[s, a, n0, k1, 1]) for n0 in range(NEAR)], -1)
                for a in range(radix)
            ]
            for k2 in range(0, NEAR, 2):
                pairs = []
                for k in (k2, k2 + 1):
                    group = []
                    for e, (re, im) in enumerate(three([quads[a][k] for a in range(radix)], -1)):
                        row = (k1 * NEAR + k) * radix + e
                        co, si = twist[0, row], twist[1, row]
                        group.append((re * co + im * si, im * co - re * si))
                    pairs.append(group)
                for e in range(radix):
                    row = (e * blocks + k1 * NEAR + k2) * SUB
                    store(s, row, [pairs[0][e], pairs[1][e]])
            yield

    def product(s):
        left, right = ((1, 0), (1, 2), (0, 2))[s]
        for row in range(0, rows, 2 * SUB):
            lr, li = spec[left, row : row + 2 * SUB, :LANES], spec[left, row : row + 2 * SUB, LANES:]
            rr, ri = spec[right, row : row + 2 * SUB, :LANES], spec[right, row : row + 2 * SUB, LANES:]
            if s == 0:
                both = lr * rr - li * ri, lr * ri + li * rr
            else:
                both = lr * rr + li * ri, lr * ri - li * rr
            for p in range(2):
                high, low = halves(both[p])
                for j, w in enumerate((high, low)):
                    lanes = (2 * j + p) * LANES
                    gs[3 + s, row : row + 2 * SUB, lanes : lanes + LANES] = w
            if row % (6 * SUB) == 0:
                yield

    def backward(s):
        for k1 in range(FAR):
            quads = []
            for k2 in range(NEAR):
                trio = []
                for e in range(radix):
                    row = (e * blocks + k1 * NEAR + k2) * SUB
                    re, im = spec[3 + s, row : row + SUB, :LANES], spec[3 + s, row : row + SUB, LANES:]
                    row = (k1 * NEAR + k2) * radix + e
                    co, si = twist[0, row], twist[1, row]
                    trio.append((re * co - im * si, im * co + re * si))
                quads.append(three(trio, 1))
            for a in range(radix):
                for n0, pair in enumerate(four([quads[k2][a] for k2 in range(NEAR)], 1)):
                    re, im = turn(pair, n0 * k1 / blocks)
                    ts[s, a, n0, k1, 0] = re
                    ts[s, a, n0, k1, 1] = im
            yield
        for a in range(radix):
            for n0 in range(NEAR):
                values = eight([(ts[s, a, n0, k1, 0], ts[s, a, n0, k1, 1]) for k1 in range(FAR)], 1)
                for n1, (re, im) in enumerate(values):
                    m = NEAR * n1 + n0
                    d = ((m - a) * pow(radix, -1, blocks)) % blocks
                    angle = 2.0 * math.pi * (radix * d + a) / (4 * span)
                    row = slots[d] * height + (a * 3 + s) * SUB
                    out[row : row + SUB, :] = (scale * math.cos(angle)) * re - (scale * math.sin(angle)) * im
                yield

    def lane_dots(s, table):
        step = rows // 3
        for row in range(0, rows, step):
            left = gs[s, row : row + step]
            main = dot(left, table[: 4 * LANES])
            spec[s, row : row + step] = main + dot(left[:, : 2 * LANES], table[4 * LANES :])
            yield

    def mix(vector, *dots):
        gap = max(1, 18 // max(1, 3 * len(dots)))
        chain = (piece for step in dots for piece in step)
        for count, _ in enumerate(vector):
            if count % gap == 0:
                next(chain, None)
        for _ in chain:
            pass

    mix(forward(0))
    mix(forward(1), lane_dots(0, lane_ahead))
    mix(forward(2), lane_dots(1, lane_ahead))
    mix(product(0), lane_dots(2, lane_ahead))
    mix(product(1), lane_dots(3, lane_behind))
    mix(product(2), lane_dots(4, lane_behind))
    mix(backward(0), lane_dots(5, lane_behind))
    mix(backward(1))
    mix(backward(2))


def unpack_kernel(
    data, gate_in, value_in, gate_out, cotangent, skip_gain, g_in, g_value, g_out, g_taps, g_skip, *, scale
):
    channels = gate_in.shape[1]
    radix = gate_in.shape[0] // LANES
    gain = skip_gain[...]
    height = 3 * radix * SUB + 1

    def piece(a, s):
        at = (a * 3 + s) * SUB
        tiles = [data[d * height + at : d * height + at + SUB, :] for d in range(channels // SUB)]
        return jnp.concatenate(tiles, axis=0).T

    for a in range(radix):
        rows = slice(a * LANES, (a + 1) * LANES)
        conv, back, lagged = (piece(a, s) for s in range(3))
        first = gate_in[rows, :].astype(jnp.float32)
        value = value_in[rows, :].astype(jnp.float32)
        second = gate_out[rows, :].astype(jnp.float32)
        grad = cotangent[rows, :].astype(jnp.float32)
        g_out[rows, :] = (grad * (conv + gain * (first * value))).astype(g_out.dtype)
        mid = back + gain * (grad * second)
        g_in[rows, :] = (mid * value).astype(g_in.dtype)
        g_value[rows, :] = (mid * first).astype(g_value.dtype)
        g_taps[rows, :] = lagged * scale
    for d in range(channels // SUB):
        share = data[(d + 1) * height - 1 : (d + 1) * height, :SUB]
        g_skip[:, d * SUB : (d + 1) * SUB] = share * scale


PARAMS = pltpu.CompilerParams(vmem_limit_bytes=24 * 1024 * 1024)
ON_CHIP = pl.BlockSpec(memory_space=pltpu.VMEM)
IN_HBM = pl.BlockSpec(memory_space=pltpu.HBM)


def held(x):
    return x if INTERPRET else pltpu.with_memory_space_constraint(x, pltpu.HBM)


def call(kernel, out_shape, scratch=(), in_specs=None):
    extra = {} if in_specs is None else {"in_specs": in_specs}
    out_specs = jax.tree.map(lambda _: ON_CHIP, out_shape)
    return pl.pallas_call(
        kernel,
        out_shape=out_shape,
        out_specs=out_specs,
        scratch_shapes=scratch,
        compiler_params=PARAMS,
        interpret=INTERPRET,
        **extra,
    )


def pack(gate_in, value_in, gate_out, cotangent, taps):
    rows, channels = taps.shape
    height = 3 * rows // LANES * SUB
    shape = jax.ShapeDtypeStruct((channels // SUB, height, LANES), jnp.float32)
    operands = tuple(held(x) for x in (taps, gate_in, value_in, cotangent, gate_out))
    scratch = [pltpu.VMEM(x.shape, x.dtype) for x in operands]
    scratch.append(pltpu.SemaphoreType.DMA((len(operands),)))
    return call(pack_kernel, shape, scratch, [IN_HBM] * len(operands))(*operands)


def spectral(data, slots):
    blocks = data.shape[0]
    radix = data.shape[1] // (3 * SUB)
    consts = [jnp.asarray(t) for t in tables(blocks, radix)]
    shape = jax.ShapeDtypeStruct((blocks * (3 * radix * SUB + 1), LANES), jnp.float32)
    rows = blocks * radix * SUB
    scratch = [
        pltpu.VMEM((3, radix, NEAR, FAR, 2, SUB, LANES), jnp.float32),
        pltpu.VMEM((6, rows, 4 * LANES), jnp.bfloat16),
        pltpu.VMEM((6, rows, 2 * LANES), jnp.float32),
    ]

    def kernel(*refs):
        spectral_kernel(*refs, slots=slots)

    return call(kernel, shape, scratch)(data, *consts)


def unpack(data, gate_in, value_in, gate_out, cotangent, skip_gain, scale):
    rows, channels = gate_in.shape
    half = jax.ShapeDtypeStruct((rows, channels), jnp.bfloat16)
    shapes = (
        half,
        half,
        half,
        jax.ShapeDtypeStruct((rows, channels), jnp.float32),
        jax.ShapeDtypeStruct((1, channels), jnp.float32),
    )

    def kernel(*refs):
        unpack_kernel(*refs, scale=scale)

    outs = call(kernel, shapes)(data, gate_in, value_in, gate_out, cotangent, skip_gain[None])
    return (*outs[:4], outs[4][0])


def body(gate_in, value_in, gate_out, filter_taps, skip_gain, cotangent):
    scale = 1.0 / math.sqrt(lax.axis_size(AXES) * gate_in.shape[0])
    data = pack(gate_in, value_in, gate_out, cotangent, filter_taps)
    data = lax.all_to_all(data, AXES, split_axis=0, concat_axis=0, tiled=True)
    sizes = [lax.axis_size(name) for name in PLACE]
    order = [PLACE.index(name) for name in AXES]
    slots = np.arange(math.prod(sizes)).reshape([sizes[i] for i in order])
    slots = [int(i) for i in slots.transpose(np.argsort(order)).reshape(-1)]
    data = spectral(data, slots)
    rows = data.reshape(lax.axis_size(AXES), -1, 1, LANES)
    data = lax.all_to_all(rows, AXES, split_axis=0, concat_axis=0, tiled=True).reshape(data.shape)
    return unpack(data, gate_in, value_in, gate_out, cotangent, skip_gain, scale)


def solution(mesh):
    near = 2
    grp, blk, ch = (mesh.shape[name] for name in ("grp", "blk", "ch"))
    split = jax.sharding.Mesh(mesh.devices.reshape(grp, blk // near, near, ch), (*PLACE, "ch"))
    spread = P(PLACE, "ch")
    return jax.shard_map(
        body,
        mesh=split,
        in_specs=(spread, spread, spread, spread, P("ch"), spread),
        out_specs=(spread, spread, spread, spread, P("ch")),
        check_vma=False,
    )
```

```python
import math

import jax
import jax.numpy as jnp
import numpy as np
from jax import lax
from jax.experimental import pallas as pl
from jax.experimental.pallas import tpu as pltpu
from jax.sharding import PartitionSpec as P

AXES = ("grp", "blk")
LANES = 128
SUB = 8
INTERPRET = False


def split_table(table):
    high = table.astype(jnp.bfloat16)
    low = (table - high.astype(np.float64)).astype(jnp.bfloat16)
    return np.concatenate([high, high, low], axis=0)


NEAR, FAR = 4, 8


def tables(blocks, radix):
    total = blocks * radix * LANES
    lane = np.arange(LANES)
    inner = 2.0 * np.pi * np.outer(lane, lane) / LANES
    cosine, sine = np.cos(inner), np.sin(inner)
    lane_ahead = np.block([[cosine, -sine], [sine, cosine]])
    lane_behind = np.block([[cosine, sine], [-sine, cosine]])
    far, near, piece = np.meshgrid(np.arange(FAR), np.arange(NEAR), np.arange(radix), indexing="ij")
    span = blocks * radix
    from_piece = blocks * pow(blocks, -1, radix) * pow(radix - 1, -1, radix)
    from_block = radix * pow(radix, -1, blocks) * radix
    key = (from_piece * piece + from_block * (far + FAR * near)) % span
    fine = 2.0 * np.pi * (key.reshape(-1, 1) + 0.25) * lane / total
    twist = np.stack([np.cos(fine), np.sin(fine)]).astype(np.float32)
    twist = np.repeat(twist[:, :, None, :], SUB, axis=2)
    return split_table(lane_ahead), split_table(lane_behind), twist


def halves(values):
    high = values.astype(jnp.bfloat16)
    low = (values - high.astype(jnp.float32)).astype(jnp.bfloat16)
    return high, low


def dot(a, b):
    return jnp.dot(a, b, preferred_element_type=jnp.float32)


def turn(pair, angle):
    re, im = pair
    eighth = round(angle * 8) % 8
    if abs(angle * 8 - round(angle * 8)) < 1e-9:
        if eighth == 0:
            return re, im
        if eighth == 2:
            return -im, re
        if eighth == 4:
            return -re, -im
        if eighth == 6:
            return im, -re
        root = math.sqrt(0.5)
        if eighth == 1:
            return root * (re - im), root * (re + im)
        if eighth == 3:
            return -root * (re + im), root * (re - im)
        if eighth == 5:
            return root * (im - re), -root * (re + im)
        return root * (re + im), root * (im - re)
    c, s = math.cos(2.0 * math.pi * angle), math.sin(2.0 * math.pi * angle)
    return c * re - s * im, c * im + s * re


def plus(x, y):
    return x[0] + y[0], x[1] + y[1]


def minus(x, y):
    return x[0] - y[0], x[1] - y[1]


def plus_i(x, y, sign):
    if sign > 0:
        return x[0] - y[1], x[1] + y[0]
    return x[0] + y[1], x[1] - y[0]


def four(x, sign):
    p, m = plus(x[0], x[2]), minus(x[0], x[2])
    q, n = plus(x[1], x[3]), minus(x[1], x[3])
    return [plus(p, q), plus_i(m, n, sign), minus(p, q), plus_i(m, n, -sign)]


def eight(x, sign):
    even, odd = four(x[0::2], sign), four(x[1::2], sign)
    odd = [odd[0]] + [turn(odd[k], sign * k / 8) for k in (1, 2, 3)]
    return [plus(even[k], odd[k]) for k in range(4)] + [minus(even[k], odd[k]) for k in range(4)]


def three(x, sign):
    total, gap = plus(x[1], x[2]), minus(x[1], x[2])
    half_root = math.sqrt(0.75)
    mid = x[0][0] - 0.5 * total[0], x[0][1] - 0.5 * total[1]
    gap = half_root * gap[0], half_root * gap[1]
    return [plus(x[0], total), plus_i(mid, gap, sign), plus_i(mid, gap, -sign)]


def pack_kernel(taps_in, gate_in, value_in, cotangent_in, gate_out_in, out, *scratch):
    sources = (taps_in, gate_in, value_in, cotangent_in, gate_out_in)
    buffers, sems = scratch[:5], scratch[5]
    copies = [pltpu.make_async_copy(src, dst, sems.at[i]) for i, (src, dst) in enumerate(zip(sources, buffers))]
    for copy in copies:
        copy.start()
    radix = taps_in.shape[0] // LANES
    taps, first, value, grad, second = buffers

    def send(s, take):
        for a in range(radix):
            turned = take(slice(a * LANES, (a + 1) * LANES)).T
            at = (a * 3 + s) * SUB
            out[:, at : at + SUB, :] = turned.reshape(-1, SUB, LANES)

    copies[0].wait()
    send(1, lambda r: taps[r, :])
    copies[1].wait()
    copies[2].wait()
    send(0, lambda r: first[r, :].astype(jnp.float32) * value[r, :].astype(jnp.float32))
    copies[3].wait()
    copies[4].wait()
    send(2, lambda r: grad[r, :].astype(jnp.float32) * second[r, :].astype(jnp.float32))


def spectral_kernel(data, lane_ahead, lane_behind, twist, out, ts, gs, spec):
    blocks = data.shape[0]
    radix = data.shape[1] // (3 * SUB)
    span = blocks * radix
    scale = 1.0 / (span * LANES)
    height = 3 * radix * SUB + 1
    rows = span * SUB

    def at(a, s):
        return slice((a * 3 + s) * SUB, (a * 3 + s + 1) * SUB)

    total = jnp.zeros((SUB, LANES), jnp.float32)
    for a in range(radix):
        total = total + jnp.sum(data[:, at(a, 0), :] * data[:, at(a, 2), :], axis=0)
    share = jnp.concatenate([jnp.sum(total.T, axis=0, keepdims=True)] * (LANES // SUB), axis=1)
    for d in range(blocks):
        out[d * height + height - 1 : (d + 1) * height, :] = share

    def store(s, row, pairs):
        for p in range(2):
            high, low = halves(jnp.concatenate([pair[p] for pair in pairs], axis=0))
            for j, w in enumerate((high, low)):
                lanes = (2 * j + p) * LANES
                gs[s, row : row + 2 * SUB, lanes : lanes + LANES] = w

    def forward(s):
        for a in range(radix):
            for n0 in range(NEAR):
                values = []
                for n1 in range(FAR):
                    m = NEAR * n1 + n0
                    d = ((m - a) * pow(radix, -1, blocks)) % blocks
                    x = data[d, at(a, s), :]
                    angle = 2.0 * math.pi * (radix * d + a) / (4 * span)
                    values.append((math.cos(angle) * x, -math.sin(angle) * x))
                for k1, pair in enumerate(eight(values, -1)):
                    re, im = turn(pair, -n0 * k1 / blocks)
                    ts[s, a, n0, k1, 0] = re
                    ts[s, a, n0, k1, 1] = im
                yield
        for k1 in range(FAR):
            quads = [
                four([(ts[s, a, n0, k1, 0], ts[s, a, n0, k1, 1]) for n0 in range(NEAR)], -1)
                for a in range(radix)
            ]
            for k2 in range(0, NEAR, 2):
                pairs = []
                for k in (k2, k2 + 1):
                    group = []
                    for e, (re, im) in enumerate(three([quads[a][k] for a in range(radix)], -1)):
                        row = (k1 * NEAR + k) * radix + e
                        co, si = twist[0, row], twist[1, row]
                        group.append((re * co + im * si, im * co - re * si))
                    pairs.append(group)
                for e in range(radix):
                    row = (e * blocks + k1 * NEAR + k2) * SUB
                    store(s, row, [pairs[0][e], pairs[1][e]])
            yield

    def product(s):
        left, right = ((1, 0), (1, 2), (0, 2))[s]
        for row in range(0, rows, 2 * SUB):
            lr, li = spec[left, row : row + 2 * SUB, :LANES], spec[left, row : row + 2 * SUB, LANES:]
            rr, ri = spec[right, row : row + 2 * SUB, :LANES], spec[right, row : row + 2 * SUB, LANES:]
            if s == 0:
                both = lr * rr - li * ri, lr * ri + li * rr
            else:
                both = lr * rr + li * ri, lr * ri - li * rr
            for p in range(2):
                high, low = halves(both[p])
                for j, w in enumerate((high, low)):
                    lanes = (2 * j + p) * LANES
                    gs[3 + s, row : row + 2 * SUB, lanes : lanes + LANES] = w
            if row % (6 * SUB) == 0:
                yield

    def backward(s):
        for k1 in range(FAR):
            quads = []
            for k2 in range(NEAR):
                trio = []
                for e in range(radix):
                    row = (e * blocks + k1 * NEAR + k2) * SUB
                    re, im = spec[3 + s, row : row + SUB, :LANES], spec[3 + s, row : row + SUB, LANES:]
                    row = (k1 * NEAR + k2) * radix + e
                    co, si = twist[0, row], twist[1, row]
                    trio.append((re * co - im * si, im * co + re * si))
                quads.append(three(trio, 1))
            for a in range(radix):
                for n0, pair in enumerate(four([quads[k2][a] for k2 in range(NEAR)], 1)):
                    re, im = turn(pair, n0 * k1 / blocks)
                    ts[s, a, n0, k1, 0] = re
                    ts[s, a, n0, k1, 1] = im
            yield
        for a in range(radix):
            for n0 in range(NEAR):
                values = eight([(ts[s, a, n0, k1, 0], ts[s, a, n0, k1, 1]) for k1 in range(FAR)], 1)
                for n1, (re, im) in enumerate(values):
                    m = NEAR * n1 + n0
                    d = ((m - a) * pow(radix, -1, blocks)) % blocks
                    angle = 2.0 * math.pi * (radix * d + a) / (4 * span)
                    row = d * height + (a * 3 + s) * SUB
                    out[row : row + SUB, :] = (scale * math.cos(angle)) * re - (scale * math.sin(angle)) * im
                yield

    def lane_dots(s, table):
        step = rows // 3
        for row in range(0, rows, step):
            left = gs[s, row : row + step]
            main = dot(left, table[: 4 * LANES])
            spec[s, row : row + step] = main + dot(left[:, : 2 * LANES], table[4 * LANES :])
            yield

    def mix(vector, *dots):
        gap = max(1, 18 // max(1, 3 * len(dots)))
        chain = (piece for step in dots for piece in step)
        for count, _ in enumerate(vector):
            if count % gap == 0:
                next(chain, None)
        for _ in chain:
            pass

    mix(forward(0))
    mix(forward(1), lane_dots(0, lane_ahead))
    mix(forward(2), lane_dots(1, lane_ahead))
    mix(product(0), lane_dots(2, lane_ahead))
    mix(product(1), lane_dots(3, lane_behind))
    mix(product(2), lane_dots(4, lane_behind))
    mix(backward(0), lane_dots(5, lane_behind))
    mix(backward(1))
    mix(backward(2))


def unpack_kernel(
    data, gate_in, value_in, gate_out, cotangent, skip_gain, g_in, g_value, g_out, g_taps, g_skip, *, scale
):
    channels = gate_in.shape[1]
    radix = gate_in.shape[0] // LANES
    gain = skip_gain[...]
    height = 3 * radix * SUB + 1

    def piece(a, s):
        at = (a * 3 + s) * SUB
        tiles = [data[d * height + at : d * height + at + SUB, :] for d in range(channels // SUB)]
        return jnp.concatenate(tiles, axis=0).T

    for a in range(radix):
        rows = slice(a * LANES, (a + 1) * LANES)
        conv, back, lagged = (piece(a, s) for s in range(3))
        first = gate_in[rows, :].astype(jnp.float32)
        value = value_in[rows, :].astype(jnp.float32)
        second = gate_out[rows, :].astype(jnp.float32)
        grad = cotangent[rows, :].astype(jnp.float32)
        g_out[rows, :] = (grad * (conv + gain * (first * value))).astype(g_out.dtype)
        mid = back + gain * (grad * second)
        g_in[rows, :] = (mid * value).astype(g_in.dtype)
        g_value[rows, :] = (mid * first).astype(g_value.dtype)
        g_taps[rows, :] = lagged * scale
    owner = lax.broadcasted_iota(jnp.int32, (1, LANES), 1) // SUB
    group = LANES // SUB
    for h in range(channels // LANES):
        picked = jnp.zeros((1, LANES), jnp.float32)
        for j in range(group):
            end = (h * group + j + 1) * height
            picked = jnp.where(owner == j, data[end - 1 : end, :], picked)
        g_skip[:, h * LANES : (h + 1) * LANES] = picked * scale


PARAMS = pltpu.CompilerParams(vmem_limit_bytes=24 * 1024 * 1024)
ON_CHIP = pl.BlockSpec(memory_space=pltpu.VMEM)
IN_HBM = pl.BlockSpec(memory_space=pltpu.HBM)


def held(x):
    return x if INTERPRET else pltpu.with_memory_space_constraint(x, pltpu.HBM)


def call(kernel, out_shape, scratch=(), in_specs=None):
    extra = {} if in_specs is None else {"in_specs": in_specs}
    out_specs = jax.tree.map(lambda _: ON_CHIP, out_shape)
    return pl.pallas_call(
        kernel,
        out_shape=out_shape,
        out_specs=out_specs,
        scratch_shapes=scratch,
        compiler_params=PARAMS,
        interpret=INTERPRET,
        **extra,
    )


def pack(gate_in, value_in, gate_out, cotangent, taps):
    rows, channels = taps.shape
    height = 3 * rows // LANES * SUB
    shape = jax.ShapeDtypeStruct((channels // SUB, height, LANES), jnp.float32)
    operands = tuple(held(x) for x in (taps, gate_in, value_in, cotangent, gate_out))
    scratch = [pltpu.VMEM(x.shape, x.dtype) for x in operands]
    scratch.append(pltpu.SemaphoreType.DMA((len(operands),)))
    return call(pack_kernel, shape, scratch, [IN_HBM] * len(operands))(*operands)


def spectral(data):
    blocks = data.shape[0]
    radix = data.shape[1] // (3 * SUB)
    consts = [jnp.asarray(t) for t in tables(blocks, radix)]
    shape = jax.ShapeDtypeStruct((blocks * (3 * radix * SUB + 1), LANES), jnp.float32)
    rows = blocks * radix * SUB
    scratch = [
        pltpu.VMEM((3, radix, NEAR, FAR, 2, SUB, LANES), jnp.float32),
        pltpu.VMEM((6, rows, 4 * LANES), jnp.bfloat16),
        pltpu.VMEM((6, rows, 2 * LANES), jnp.float32),
    ]
    return call(spectral_kernel, shape, scratch)(data, *consts)


def unpack(data, gate_in, value_in, gate_out, cotangent, skip_gain, scale):
    rows, channels = gate_in.shape
    half = jax.ShapeDtypeStruct((rows, channels), jnp.bfloat16)
    shapes = (
        half,
        half,
        half,
        jax.ShapeDtypeStruct((rows, channels), jnp.float32),
        jax.ShapeDtypeStruct((1, channels), jnp.float32),
    )

    def kernel(*refs):
        unpack_kernel(*refs, scale=scale)

    outs = call(kernel, shapes)(data, gate_in, value_in, gate_out, cotangent, skip_gain[None])
    return (*outs[:4], outs[4][0])


def body(gate_in, value_in, gate_out, filter_taps, skip_gain, cotangent):
    scale = 1.0 / math.sqrt(lax.axis_size(AXES) * gate_in.shape[0])
    data = pack(gate_in, value_in, gate_out, cotangent, filter_taps)
    data = lax.all_to_all(data, AXES, split_axis=0, concat_axis=0, tiled=True)
    data = spectral(data)
    rows = data.reshape(lax.axis_size(AXES), -1, 1, LANES)
    data = lax.all_to_all(rows, AXES, split_axis=0, concat_axis=0, tiled=True).reshape(data.shape)
    return unpack(data, gate_in, value_in, gate_out, cotangent, skip_gain, scale)


def solution(mesh):
    spread = P(AXES, "ch")
    return jax.shard_map(
        body,
        mesh=mesh,
        in_specs=(spread, spread, spread, spread, P("ch"), spread),
        out_specs=(spread, spread, spread, spread, P("ch")),
        check_vma=False,
    )
```

```python
import math

import jax
import jax.numpy as jnp
import numpy as np
from jax import lax
from jax.experimental import pallas as pl
from jax.experimental.pallas import tpu as pltpu
from jax.sharding import PartitionSpec as P

AXES = ("grp", "blk")
LANES = 128
SUB = 8
INTERPRET = False


def split_table(table):
    high = table.astype(jnp.bfloat16)
    low = (table - high.astype(np.float64)).astype(jnp.bfloat16)
    return np.concatenate([high, high, low], axis=0)


NEAR, FAR = 4, 8


def tables(blocks, radix):
    total = blocks * radix * LANES
    lane = np.arange(LANES)
    inner = 2.0 * np.pi * np.outer(lane, lane) / LANES
    cosine, sine = np.cos(inner), np.sin(inner)
    lane_ahead = np.block([[cosine, -sine], [sine, cosine]])
    lane_behind = np.block([[cosine, sine], [-sine, cosine]])
    far, near, piece = np.meshgrid(np.arange(FAR), np.arange(NEAR), np.arange(radix), indexing="ij")
    span = blocks * radix
    from_piece = blocks * pow(blocks, -1, radix) * pow(radix - 1, -1, radix)
    from_block = radix * pow(radix, -1, blocks) * radix
    key = (from_piece * piece + from_block * (far + FAR * near)) % span
    fine = 2.0 * np.pi * (key.reshape(-1, 1) + 0.25) * lane / total
    twist = np.stack([np.cos(fine), np.sin(fine)]).astype(np.float32)
    twist = np.repeat(twist[:, :, None, :], SUB, axis=2)
    return split_table(lane_ahead), split_table(lane_behind), twist


def halves(values):
    high = values.astype(jnp.bfloat16)
    low = (values - high.astype(jnp.float32)).astype(jnp.bfloat16)
    return high, low


def dot(a, b):
    return jnp.dot(a, b, preferred_element_type=jnp.float32)


def turn(pair, angle):
    re, im = pair
    eighth = round(angle * 8) % 8
    if abs(angle * 8 - round(angle * 8)) < 1e-9:
        if eighth == 0:
            return re, im
        if eighth == 2:
            return -im, re
        if eighth == 4:
            return -re, -im
        if eighth == 6:
            return im, -re
        root = math.sqrt(0.5)
        if eighth == 1:
            return root * (re - im), root * (re + im)
        if eighth == 3:
            return -root * (re + im), root * (re - im)
        if eighth == 5:
            return root * (im - re), -root * (re + im)
        return root * (re + im), root * (im - re)
    c, s = math.cos(2.0 * math.pi * angle), math.sin(2.0 * math.pi * angle)
    return c * re - s * im, c * im + s * re


def plus(x, y):
    return x[0] + y[0], x[1] + y[1]


def minus(x, y):
    return x[0] - y[0], x[1] - y[1]


def plus_i(x, y, sign):
    if sign > 0:
        return x[0] - y[1], x[1] + y[0]
    return x[0] + y[1], x[1] - y[0]


def four(x, sign):
    p, m = plus(x[0], x[2]), minus(x[0], x[2])
    q, n = plus(x[1], x[3]), minus(x[1], x[3])
    return [plus(p, q), plus_i(m, n, sign), minus(p, q), plus_i(m, n, -sign)]


def eight(x, sign):
    even, odd = four(x[0::2], sign), four(x[1::2], sign)
    odd = [odd[0]] + [turn(odd[k], sign * k / 8) for k in (1, 2, 3)]
    return [plus(even[k], odd[k]) for k in range(4)] + [minus(even[k], odd[k]) for k in range(4)]


def three(x, sign):
    total, gap = plus(x[1], x[2]), minus(x[1], x[2])
    half_root = math.sqrt(0.75)
    mid = x[0][0] - 0.5 * total[0], x[0][1] - 0.5 * total[1]
    gap = half_root * gap[0], half_root * gap[1]
    return [plus(x[0], total), plus_i(mid, gap, sign), plus_i(mid, gap, -sign)]


def pack_kernel(taps_in, gate_in, value_in, cotangent_in, gate_out_in, out, *scratch):
    sources = (taps_in, gate_in, value_in, cotangent_in, gate_out_in)
    buffers, sems = scratch[:5], scratch[5]
    copies = [pltpu.make_async_copy(src, dst, sems.at[i]) for i, (src, dst) in enumerate(zip(sources, buffers))]
    half = taps_in.shape[0] // 2
    upper, lower = pl.ds(0, half), pl.ds(half, taps_in.shape[0] - half)
    copies[0] = pltpu.make_async_copy(taps_in.at[upper], buffers[0].at[upper], sems.at[0])
    tail = pltpu.make_async_copy(taps_in.at[lower], buffers[0].at[lower], sems.at[5])
    for copy in (copies[0], tail, *copies[1:]):
        copy.start()
    radix = taps_in.shape[0] // LANES
    taps, first, value, grad, second = buffers

    def send(s, take):
        for a in range(radix):
            turned = take(slice(a * LANES, (a + 1) * LANES)).T
            at = (a * 3 + s) * SUB
            out[:, at : at + SUB, :] = turned.reshape(-1, SUB, LANES)

    copies[0].wait()
    tail.wait()
    send(1, lambda r: taps[r, :])
    copies[1].wait()
    copies[2].wait()
    send(0, lambda r: first[r, :].astype(jnp.float32) * value[r, :].astype(jnp.float32))
    copies[3].wait()
    copies[4].wait()
    send(2, lambda r: grad[r, :].astype(jnp.float32) * second[r, :].astype(jnp.float32))


def spectral_kernel(data, lane_ahead, lane_behind, twist, out, ts, gs, spec):
    blocks = data.shape[0]
    radix = data.shape[1] // (3 * SUB)
    span = blocks * radix
    scale = 1.0 / (span * LANES)
    height = 3 * radix * SUB + 1
    rows = span * SUB

    def at(a, s):
        return slice((a * 3 + s) * SUB, (a * 3 + s + 1) * SUB)

    total = jnp.zeros((SUB, LANES), jnp.float32)
    for a in range(radix):
        total = total + jnp.sum(data[:, at(a, 0), :] * data[:, at(a, 2), :], axis=0)
    share = jnp.concatenate([jnp.sum(total.T, axis=0, keepdims=True)] * (LANES // SUB), axis=1)
    for d in range(blocks):
        out[d * height + height - 1 : (d + 1) * height, :] = share

    def store(s, row, pairs):
        for p in range(2):
            high, low = halves(jnp.concatenate([pair[p] for pair in pairs], axis=0))
            for j, w in enumerate((high, low)):
                lanes = (2 * j + p) * LANES
                gs[s, row : row + 2 * SUB, lanes : lanes + LANES] = w

    def forward(s):
        for a in range(radix):
            for n0 in range(NEAR):
                values = []
                for n1 in range(FAR):
                    m = NEAR * n1 + n0
                    d = ((m - a) * pow(radix, -1, blocks)) % blocks
                    x = data[d, at(a, s), :]
                    angle = 2.0 * math.pi * (radix * d + a) / (4 * span)
                    values.append((math.cos(angle) * x, -math.sin(angle) * x))
                for k1, pair in enumerate(eight(values, -1)):
                    re, im = turn(pair, -n0 * k1 / blocks)
                    ts[s, a, n0, k1, 0] = re
                    ts[s, a, n0, k1, 1] = im
                yield
        for k1 in range(FAR):
            quads = [
                four([(ts[s, a, n0, k1, 0], ts[s, a, n0, k1, 1]) for n0 in range(NEAR)], -1)
                for a in range(radix)
            ]
            for k2 in range(0, NEAR, 2):
                pairs = []
                for k in (k2, k2 + 1):
                    group = []
                    for e, (re, im) in enumerate(three([quads[a][k] for a in range(radix)], -1)):
                        row = (k1 * NEAR + k) * radix + e
                        co, si = twist[0, row], twist[1, row]
                        group.append((re * co + im * si, im * co - re * si))
                    pairs.append(group)
                for e in range(radix):
                    row = (e * blocks + k1 * NEAR + k2) * SUB
                    store(s, row, [pairs[0][e], pairs[1][e]])
            yield

    def product(s):
        left, right = ((1, 0), (1, 2), (0, 2))[s]
        for row in range(0, rows, 2 * SUB):
            lr, li = spec[left, row : row + 2 * SUB, :LANES], spec[left, row : row + 2 * SUB, LANES:]
            rr, ri = spec[right, row : row + 2 * SUB, :LANES], spec[right, row : row + 2 * SUB, LANES:]
            if s == 0:
                both = lr * rr - li * ri, lr * ri + li * rr
            else:
                both = lr * rr + li * ri, lr * ri - li * rr
            for p in range(2):
                high, low = halves(both[p])
                for j, w in enumerate((high, low)):
                    lanes = (2 * j + p) * LANES
                    gs[3 + s, row : row + 2 * SUB, lanes : lanes + LANES] = w
            if row % (6 * SUB) == 0:
                yield

    def backward(s):
        for k1 in range(FAR):
            quads = []
            for k2 in range(NEAR):
                trio = []
                for e in range(radix):
                    row = (e * blocks + k1 * NEAR + k2) * SUB
                    re, im = spec[3 + s, row : row + SUB, :LANES], spec[3 + s, row : row + SUB, LANES:]
                    row = (k1 * NEAR + k2) * radix + e
                    co, si = twist[0, row], twist[1, row]
                    trio.append((re * co - im * si, im * co + re * si))
                quads.append(three(trio, 1))
            for a in range(radix):
                for n0, pair in enumerate(four([quads[k2][a] for k2 in range(NEAR)], 1)):
                    re, im = turn(pair, n0 * k1 / blocks)
                    ts[s, a, n0, k1, 0] = re
                    ts[s, a, n0, k1, 1] = im
            yield
        for a in range(radix):
            for n0 in range(NEAR):
                values = eight([(ts[s, a, n0, k1, 0], ts[s, a, n0, k1, 1]) for k1 in range(FAR)], 1)
                for n1, (re, im) in enumerate(values):
                    m = NEAR * n1 + n0
                    d = ((m - a) * pow(radix, -1, blocks)) % blocks
                    angle = 2.0 * math.pi * (radix * d + a) / (4 * span)
                    row = d * height + (a * 3 + s) * SUB
                    out[row : row + SUB, :] = (scale * math.cos(angle)) * re - (scale * math.sin(angle)) * im
                yield

    def lane_dots(s, table):
        step = rows // 3
        for row in range(0, rows, step):
            left = gs[s, row : row + step]
            main = dot(left, table[: 4 * LANES])
            spec[s, row : row + step] = main + dot(left[:, : 2 * LANES], table[4 * LANES :])
            yield

    def mix(vector, *dots):
        gap = max(1, 18 // max(1, 3 * len(dots)))
        chain = (piece for step in dots for piece in step)
        for count, _ in enumerate(vector):
            if count % gap == 0:
                next(chain, None)
        for _ in chain:
            pass

    mix(forward(0))
    mix(forward(1), lane_dots(0, lane_ahead))
    mix(forward(2), lane_dots(1, lane_ahead))
    mix(product(0), lane_dots(2, lane_ahead))
    mix(product(1), lane_dots(3, lane_behind))
    mix(product(2), lane_dots(4, lane_behind))
    mix(backward(0), lane_dots(5, lane_behind))
    mix(backward(1))
    mix(backward(2))


def unpack_kernel(
    data, gate_in, value_in, gate_out, cotangent, skip_gain, g_in, g_value, g_out, g_taps, g_skip, *, scale
):
    channels = gate_in.shape[1]
    radix = gate_in.shape[0] // LANES
    gain = skip_gain[...]
    height = 3 * radix * SUB + 1

    def piece(a, s):
        at = (a * 3 + s) * SUB
        tiles = [data[d * height + at : d * height + at + SUB, :] for d in range(channels // SUB)]
        return jnp.concatenate(tiles, axis=0).T

    for a in range(radix):
        rows = slice(a * LANES, (a + 1) * LANES)
        conv, back, lagged = (piece(a, s) for s in range(3))
        first = gate_in[rows, :].astype(jnp.float32)
        value = value_in[rows, :].astype(jnp.float32)
        second = gate_out[rows, :].astype(jnp.float32)
        grad = cotangent[rows, :].astype(jnp.float32)
        g_out[rows, :] = (grad * (conv + gain * (first * value))).astype(g_out.dtype)
        mid = back + gain * (grad * second)
        g_in[rows, :] = (mid * value).astype(g_in.dtype)
        g_value[rows, :] = (mid * first).astype(g_value.dtype)
        g_taps[rows, :] = lagged * scale
    for d in range(channels // SUB):
        share = data[(d + 1) * height - 1 : (d + 1) * height, :SUB]
        g_skip[:, d * SUB : (d + 1) * SUB] = share * scale


PARAMS = pltpu.CompilerParams(vmem_limit_bytes=24 * 1024 * 1024)
ON_CHIP = pl.BlockSpec(memory_space=pltpu.VMEM)
IN_HBM = pl.BlockSpec(memory_space=pltpu.HBM)


def held(x):
    return x if INTERPRET else pltpu.with_memory_space_constraint(x, pltpu.HBM)


def call(kernel, out_shape, scratch=(), in_specs=None):
    extra = {} if in_specs is None else {"in_specs": in_specs}
    out_specs = jax.tree.map(lambda _: ON_CHIP, out_shape)
    return pl.pallas_call(
        kernel,
        out_shape=out_shape,
        out_specs=out_specs,
        scratch_shapes=scratch,
        compiler_params=PARAMS,
        interpret=INTERPRET,
        **extra,
    )


def pack(gate_in, value_in, gate_out, cotangent, taps):
    rows, channels = taps.shape
    height = 3 * rows // LANES * SUB
    shape = jax.ShapeDtypeStruct((channels // SUB, height, LANES), jnp.float32)
    operands = tuple(held(x) for x in (taps, gate_in, value_in, cotangent, gate_out))
    scratch = [pltpu.VMEM(x.shape, x.dtype) for x in operands]
    scratch.append(pltpu.SemaphoreType.DMA((len(operands) + 1,)))
    return call(pack_kernel, shape, scratch, [IN_HBM] * len(operands))(*operands)


def spectral(data):
    blocks = data.shape[0]
    radix = data.shape[1] // (3 * SUB)
    consts = [jnp.asarray(t) for t in tables(blocks, radix)]
    shape = jax.ShapeDtypeStruct((blocks * (3 * radix * SUB + 1), LANES), jnp.float32)
    rows = blocks * radix * SUB
    scratch = [
        pltpu.VMEM((3, radix, NEAR, FAR, 2, SUB, LANES), jnp.float32),
        pltpu.VMEM((6, rows, 4 * LANES), jnp.bfloat16),
        pltpu.VMEM((6, rows, 2 * LANES), jnp.float32),
    ]
    return call(spectral_kernel, shape, scratch)(data, *consts)


def unpack(data, gate_in, value_in, gate_out, cotangent, skip_gain, scale):
    rows, channels = gate_in.shape
    half = jax.ShapeDtypeStruct((rows, channels), jnp.bfloat16)
    shapes = (
        half,
        half,
        half,
        jax.ShapeDtypeStruct((rows, channels), jnp.float32),
        jax.ShapeDtypeStruct((1, channels), jnp.float32),
    )

    def kernel(*refs):
        unpack_kernel(*refs, scale=scale)

    outs = call(kernel, shapes)(data, gate_in, value_in, gate_out, cotangent, skip_gain[None])
    return (*outs[:4], outs[4][0])


def body(gate_in, value_in, gate_out, filter_taps, skip_gain, cotangent):
    scale = 1.0 / math.sqrt(lax.axis_size(AXES) * gate_in.shape[0])
    data = pack(gate_in, value_in, gate_out, cotangent, filter_taps)
    data = lax.all_to_all(data, AXES, split_axis=0, concat_axis=0, tiled=True)
    data = spectral(data)
    rows = data.reshape(lax.axis_size(AXES), -1, 1, LANES)
    data = lax.all_to_all(rows, AXES, split_axis=0, concat_axis=0, tiled=True).reshape(data.shape)
    return unpack(data, gate_in, value_in, gate_out, cotangent, skip_gain, scale)


def solution(mesh):
    spread = P(AXES, "ch")
    return jax.shard_map(
        body,
        mesh=mesh,
        in_specs=(spread, spread, spread, spread, P("ch"), spread),
        out_specs=(spread, spread, spread, spread, P("ch")),
        check_vma=False,
    )
```
